128 devices in a mesh: req: 4 (over x), exp: 32 (over y, z, core).
Axes of the slice: x: 4, y: 4, z: 4, core: 2. Of those that a mesh axis runs over, the one named last changes fastest.
Arguments:
- tokens: bfloat16 [32768, 1536], P(('req', 'exp')), may hold values from -6 to 6
- token_request_slot: int32 [128, 256], P(('req', 'exp')), may hold values from 0 to 3, never falling along the last dimension, each value on 1 to 128 neighbouring positions
- request_prompt: int32 [512], P(('req', 'exp')), may hold values from 0 to 31
- request_adapter: int32 [512], P(('req', 'exp')), may hold values from 0 to 15
- prompt_page_table: int32 [512], replicated, may hold values from 0 to 511, each once
- shared_prompt_cache: bfloat16 [512, 16, 512], P(('req', 'exp')), may hold values from -180 to 180
- routes: int32 [32768, 4], P(('req', 'exp')), may hold values from 0 to 31, all different within a row; in each aligned block of 256 rows (0 to 255, 256 to 511, ...) at most 48 rows name the same one
- attention_norm_gain: bfloat16 [1536], replicated, may hold values from 0.099609375 to 1.8984375
- query_matrix: bfloat16 [1536, 1536], replicated, may hold values from -0.15625 to 0.15625
- key_value_weight: bfloat16 [1536, 512], replicated, may hold values from -0.15625 to 0.15625
- attention_output_weight: bfloat16 [1536, 1536], replicated, may hold values from -0.15625 to 0.15625
- adapter_query_down: bfloat16 [1536, 256], replicated, may hold values from -0.15625 to 0.15625
- adapter_query_up: bfloat16 [256, 1536], replicated, may hold values from -1.5 to 1.5
- adapter_output_down: bfloat16 [1536, 256], replicated, may hold values from -0.15625 to 0.15625
- adapter_output_up: bfloat16 [256, 1536], replicated, may hold values from -1.5 to 1.5
- expert_norm_gain: bfloat16 [1536], replicated, may hold values from 0.099609375 to 1.8984375
- router: bfloat16 [1536, 32], replicated, may hold values from -0.15625 to 0.15625
- expert_gate_up: bfloat16 [32, 1536, 1536], P('exp'), may hold values from -0.15625 to 0.15625
- expert_down: bfloat16 [32, 768, 1536], P('exp'), may hold values from -0.21875 to 0.21875
Outputs:
- mixed_rows: bfloat16 [32768, 1536], P(('req', 'exp'))
The draws below stay inside these ranges and needn't reach their ends.
Inputs may be any that keep to these rules, and one draw needn't show every extreme that they name: `token_request_slot`: along a device's row the slots never fall; each of the 4 slots holds 1 to 128 tokens and one holds exactly 128. `prompt_page_table`: the entries whose index divided by 16 (rounded down) is p are the pages of prompt p in order; every page appears once. `routes`: each token names 4 different experts. Among the tokens of one device no expert is named more than 48 times, and in every draw some device's tokens name some expert exactly 48 times.
All inputs are finite; a program needn't handle non-finite values.
Results may differ from the reference program's by a relative error of at most 0.017.
The reference program's roundings to bfloat16 on the way count: a program that leaves them out, or rounds other values in their place, can miss the bound.
Values may be sent and summed in bfloat16 or wider, within the bound.
A program may use at most 128 MiB of HBM per device.

```python
import math
import jax
import jax.numpy as jnp
import numpy as np
from jax import lax

MODEL_WIDTH = 1536
QUERY_HEADS = 12
KEY_VALUE_HEADS = 2
HEAD_WIDTH = 128
FFE = 768
TOPK = 4
ADAPTER_RANK = 16
ADAPTER_COUNT = 16
E = 32
TOK_DEV = 256
REQ_DEV = 4
SEGMOST = 128
PAGE_TOKENS = 16
PPP = 16
PROMPT_LENGTH = 256
PROMPTS = 32
CACHE_PAGES = 512
GROUPS = 128
TOKENS = 32768
REQUESTS = 512
CAP = 48


def draw_shared_prompt_cache(key, part):
    cache_layout = (CACHE_PAGES, PAGE_TOKENS, 2 * KEY_VALUE_HEADS * HEAD_WIDTH)
    values = jax.random.normal(key, cache_layout, jnp.float32)
    return jnp.clip(values, -6.0, 6.0).astype(jnp.bfloat16)


def set_ends(entries, rng, smallest, largest):
    shape = entries.shape
    place = [jax.random.randint(jax.random.fold_in(rng, axis), (), 0, shape[axis]) for axis in range(len(shape))]
    entries = entries.at[tuple(place)].set(smallest)
    longest = shape.index(max(shape))
    place[longest] = (place[longest] + 1) % shape[longest]
    return entries.at[tuple(place)].set(largest)


def shard_levels(key, dims, cuts, least, top_value):
    level = 1.0
    for dim, shards_of in cuts:
        heights = jax.random.uniform(jax.random.fold_in(jax.random.fold_in(key, 6), dim), (shards_of,), jnp.float32, least / len(cuts), top_value / len(cuts))
        level = level * jnp.repeat(jnp.exp(heights), dims[dim] // shards_of).reshape((-1,) + (1,) * (len(dims) - 1 - dim))
    return level


def length_profile(count, total, bound, lean):
    weights = [(1 << 20) // math.isqrt(rank ** lean) + 1 for rank in range(2, count + 1)]
    surplus, given = total - bound - (count - 1), [1] * (count - 1)
    while surplus > 0:
        candidates = [i for i in range(count - 1) if given[i] < bound]
        mass, remaining = sum([weights[i] for i in candidates]), surplus
        for i in candidates:
            addition = min(bound - given[i], max(1, remaining * weights[i] // mass), surplus)
            given[i] = given[i] + addition
            surplus = surplus - addition
    return np.array([bound] + given)


def ragged_sizes(key, amount, total, most, slope):
    if amount == 2:
        one = jax.random.randint(key, (), max(1, total - most), min(most, total - 1) + 1)
        return jnp.stack([one, total - one])
    lengths = jnp.asarray(length_profile(amount, total, most, slope), jnp.int32)
    twos = (amount - 1) // 2
    source_of, sink = lengths[1:1 + 2 * twos:2], lengths[2:2 + 2 * twos:2]
    room = jnp.minimum(source_of - 1, most - sink)
    passed = jax.random.randint(jax.random.fold_in(key, 1), (twos,), 0, 1 << 20) % (room + 1)
    lengths = lengths.at[1:1 + 2 * twos:2].set(source_of - passed).at[2:2 + 2 * twos:2].set(sink + passed)
    return lengths[jax.random.permutation(jax.random.fold_in(key, 2), amount)]


def routed_block(key, own, number, rows, number_of, top, bound, lean):
    ranking = jax.random.permutation(key, number_of)
    crowded, common = shares(number_of, rows * top, bound, lean, True), shares(number_of, rows * top, bound, lean, False)
    places = jnp.arange(number_of)

    def named(lengths, turn):
        used = int((lengths > 0).sum())
        fixed = max(1, used // 4)
        shifted = fixed + (places - fixed + turn * (used - fixed)) % max(1, number_of - fixed)
        return jnp.zeros((number_of,), jnp.int32).at[ranking[jnp.where(places < fixed, places, shifted)]].set(jnp.asarray(lengths, jnp.int32))

    lengths = jnp.where(number % 4 == 0, named(crowded, number // 4), named(common, number - number // 4 - 1))
    mixed = jax.random.permutation(jax.random.fold_in(own, 3), number_of)
    giver, receiver = mixed[0:number_of // 2 * 2:2], mixed[1:number_of // 2 * 2:2]
    room = jnp.minimum(lengths[giver] - 1, bound - lengths[receiver]) // 2
    room = jnp.where((giver == ranking[0]) | (receiver == ranking[0]) | (lengths[receiver] == 0), 0, jnp.maximum(room, 0))
    shifted = jax.random.randint(jax.random.fold_in(own, 4), (number_of // 2,), 0, 1 << 20) % (room + 1)
    lengths = lengths.at[giver].add(-shifted).at[receiver].add(shifted)
    members = jnp.searchsorted(jnp.cumsum(lengths), jnp.arange(rows * top), side="right").astype(jnp.int32)
    table = members.reshape(top, rows).T
    table = table[jax.random.permutation(jax.random.fold_in(own, 1), rows)]
    turn = jax.random.randint(jax.random.fold_in(own, 2), (rows, 1), 0, top)
    return jnp.take_along_axis(table, (jnp.arange(top)[None, :] + turn) % top, axis=1)


def shares(amount, total, reach, lean, full):
    portions = [(1 << 20) // math.isqrt(rank ** lean) + 1 for rank in range(1, amount + 1)]
    largest = reach if full else min(reach, max(-(-total // amount), total * portions[0] // sum(portions)))
    least = 1 if total - largest >= amount - 1 else 0
    given, surplus = [largest] + [least] * (amount - 1), total - largest - least * (amount - 1)
    while surplus > 0:
        candidates = [i for i in range(1, amount) if given[i] < largest] or [i for i in range(1, amount) if given[i] < reach]
        pool, remaining = sum([portions[i] for i in candidates]), surplus
        for i in candidates:
            more = min(reach - given[i], max(1, remaining * portions[i] // pool), surplus)
            given[i] = given[i] + more
            surplus = surplus - more
    return np.array(given)


def noise(own_key, extent, scale, limit, cuts=(), held_as=jnp.bfloat16):
    values = scale * jax.random.normal(own_key, extent, jnp.float32)
    if cuts:
        values = values * shard_levels(own_key, extent, cuts, -0.22, 0.18)
    return jnp.clip(values, -limit, limit).astype(held_as)


def setup_inputs(seed: int = 0) -> dict:
    key_of = jax.random.split(jax.random.key(seed), 20)
    tokens = noise(key_of[0], (TOKENS, MODEL_WIDTH), 1.0, 6.0, ((0, 128),))
    token_request_slot = jax.vmap(lambda own: jnp.searchsorted(jnp.cumsum(ragged_sizes(own, REQ_DEV, TOK_DEV, SEGMOST, 2)), jnp.arange(TOK_DEV), side="right"))(jax.random.split(key_of[1], GROUPS)).reshape((GROUPS, TOK_DEV)).astype(jnp.int32)
    request_prompt = set_ends(jax.random.randint(key_of[2], (REQUESTS,), 0, PROMPTS), jax.random.fold_in(key_of[2], 1), 0, PROMPTS - 1).astype(jnp.int32)
    request_adapter = set_ends(jax.random.randint(key_of[3], (REQUESTS,), 0, ADAPTER_COUNT), jax.random.fold_in(key_of[3], 1), 0, ADAPTER_COUNT - 1).astype(jnp.int32)
    prompt_page_table = jax.random.permutation(key_of[4], CACHE_PAGES).astype(jnp.int32)
    shared_prompt_cache = draw_shared_prompt_cache(jax.random.fold_in(key_of[19], 71), 0)
    routes_keys = jax.random.split(jax.random.fold_in(key_of[6], 1), TOKENS // TOK_DEV)
    routes_turns = jax.random.permutation(jax.random.fold_in(key_of[6], 3), TOKENS // TOK_DEV)
    routes = jax.vmap(lambda own, number: routed_block(jax.random.fold_in(key_of[6], 2), own, number, TOK_DEV, E, TOPK, CAP, 1))(routes_keys, routes_turns).reshape((TOKENS, TOPK))
    attention_norm_gain = jnp.clip(1.0 + 0.18 * jax.random.normal(key_of[7], (MODEL_WIDTH,), jnp.float32), 0.099609375, 1.8984375).astype(jnp.bfloat16)
    query_matrix = noise(key_of[8], (MODEL_WIDTH, QUERY_HEADS * HEAD_WIDTH), MODEL_WIDTH ** -0.5, 0.15625)
    key_value_weight = noise(key_of[9], (MODEL_WIDTH, 2 * KEY_VALUE_HEADS * HEAD_WIDTH), MODEL_WIDTH ** -0.5, 0.15625)
    attention_output_weight = noise(key_of[10], (QUERY_HEADS * HEAD_WIDTH, MODEL_WIDTH), (QUERY_HEADS * HEAD_WIDTH) ** -0.5, 0.15625)
    adapter_query_down = noise(key_of[11], (MODEL_WIDTH, ADAPTER_COUNT * ADAPTER_RANK), MODEL_WIDTH ** -0.5, 0.15625)
    adapter_query_up = noise(key_of[12], (ADAPTER_COUNT * ADAPTER_RANK, QUERY_HEADS * HEAD_WIDTH), ADAPTER_RANK ** -0.5, 1.5)
    adapter_output_down = noise(key_of[13], (QUERY_HEADS * HEAD_WIDTH, ADAPTER_COUNT * ADAPTER_RANK), (QUERY_HEADS * HEAD_WIDTH) ** -0.5, 0.15625)
    adapter_output_up = noise(key_of[14], (ADAPTER_COUNT * ADAPTER_RANK, MODEL_WIDTH), ADAPTER_RANK ** -0.5, 1.5)
    expert_norm_gain = jnp.clip(1.0 + 0.18 * jax.random.normal(key_of[15], (MODEL_WIDTH,), jnp.float32), 0.099609375, 1.8984375).astype(jnp.bfloat16)
    router = noise(key_of[16], (MODEL_WIDTH, E), MODEL_WIDTH ** -0.5, 0.15625)
    expert_gate_up = noise(key_of[17], (E, MODEL_WIDTH, 2 * FFE), MODEL_WIDTH ** -0.5, 0.15625, ((0, 32),))
    expert_down = noise(key_of[18], (E, FFE, MODEL_WIDTH), FFE ** -0.5, 0.21875, ((0, 32),))
    return dict(tokens=tokens, token_request_slot=token_request_slot, request_prompt=request_prompt, request_adapter=request_adapter, prompt_page_table=prompt_page_table, shared_prompt_cache=shared_prompt_cache, routes=routes, attention_norm_gain=attention_norm_gain, query_matrix=query_matrix, key_value_weight=key_value_weight, attention_output_weight=attention_output_weight, adapter_query_down=adapter_query_down, adapter_query_up=adapter_query_up, adapter_output_down=adapter_output_down, adapter_output_up=adapter_output_up, expert_norm_gain=expert_norm_gain, router=router, expert_gate_up=expert_gate_up, expert_down=expert_down)


EPSILON = 1e-06
THETA = 1000000.0
VERY_NEGATIVE = -1e+30

def rms_norm(weight_matrix, gain_vector):
    values = weight_matrix.astype(jnp.float32)
    factor = lax.rsqrt(lax.optimization_barrier(jnp.mean(values * values, axis=-1, keepdims=True)) + EPSILON)
    return (values * factor * gain_vector.astype(jnp.float32)).astype(jnp.bfloat16)

def apply_rotary(values, token_positions):
    half_width = values.shape[-1] // 2
    frequency = THETA ** (-jnp.arange(half_width).astype(jnp.float32) / half_width)
    angles = token_positions.astype(jnp.float32)[:, None] * frequency[None, :]
    cosine = jnp.cos(angles)[:, None, :]
    sine_table = jnp.sin(angles)[:, None, :]
    first_half = values[..., :half_width]
    second = values[..., half_width:]
    return jnp.concatenate([first_half * cosine - second * sine_table, second * cosine + first_half * sine_table], axis=-1)

def adapter_update(weight_matrix, down_proj, up_proj, token_adapter):
    inner = jnp.dot(weight_matrix, down_proj, preferred_element_type=jnp.float32)
    owner_slot = jnp.arange(down_proj.shape[1], dtype=jnp.int32) // ADAPTER_RANK
    inner = jnp.where(owner_slot[None, :] == token_adapter[:, None], inner, 0.0).astype(jnp.bfloat16)
    return jnp.dot(inner, up_proj, preferred_element_type=jnp.float32)

def request_info(request_row, prompt_req, adapter_req):
    new_token_count = request_row.shape[0]
    request_slot_count = prompt_req.shape[0]
    matches = request_row[:, None] == jnp.arange(request_slot_count, dtype=jnp.int32)[None, :]
    token_adapter = lax.optimization_barrier(jnp.sum(jnp.where(matches, adapter_req[None, :], 0), axis=1)).astype(jnp.int32)
    prompt_tok = lax.optimization_barrier(jnp.sum(jnp.where(matches, prompt_req[None, :], 0), axis=1)).astype(jnp.int32)
    token_index = jnp.arange(new_token_count, dtype=jnp.int32)
    first_row = lax.optimization_barrier(jnp.min(jnp.where(matches, token_index[:, None], new_token_count), axis=0)).astype(jnp.int32)
    start_tok = lax.optimization_barrier(jnp.sum(jnp.where(matches, first_row[None, :], 0), axis=1)).astype(jnp.int32)
    token_positions = (PROMPT_LENGTH + token_index - start_tok).astype(jnp.int32)
    return (token_adapter, prompt_tok, token_positions)

def apply_projection(tokens, token_adapter, token_positions, attention_norm_gain, query_matrix, key_value_weight, adapter_query_down, adapter_query_up):
    new_token_count = tokens.shape[0]
    normalized = rms_norm(tokens, attention_norm_gain)
    query_rows = jnp.dot(normalized, query_matrix, preferred_element_type=jnp.float32)
    query_rows = query_rows + adapter_update(normalized, adapter_query_down, adapter_query_up, token_adapter)
    query_rows = apply_rotary(query_rows.reshape(new_token_count, QUERY_HEADS, HEAD_WIDTH), token_positions).astype(jnp.bfloat16)
    key_value_rows = jnp.dot(normalized, key_value_weight, preferred_element_type=jnp.float32).reshape(new_token_count, 2 * KEY_VALUE_HEADS, HEAD_WIDTH)
    key_matrix = apply_rotary(key_value_rows[:, :KEY_VALUE_HEADS], token_positions).astype(jnp.bfloat16)
    value_matrix = key_value_rows[:, KEY_VALUE_HEADS:].astype(jnp.bfloat16)
    return (query_rows, key_matrix, value_matrix)

def finalize(attention_output, tokens, token_adapter, attention_output_weight, adapter_output_down, adapter_output_up):
    expert_mixture = jnp.dot(attention_output, attention_output_weight, preferred_element_type=jnp.float32)
    expert_mixture = expert_mixture + adapter_update(attention_output, adapter_output_down, adapter_output_up, token_adapter)
    return (tokens.astype(jnp.float32) + expert_mixture).astype(jnp.bfloat16)

def gate_weights(ffn_normed, router, routes):
    logits = jnp.dot(ffn_normed, router, preferred_element_type=jnp.float32)
    picked = jnp.take_along_axis(logits, routes, axis=1)
    squashed = jax.nn.sigmoid(picked)
    return squashed / lax.optimization_barrier(jnp.sum(squashed, axis=1, keepdims=True))

def slot_of(routes, experts, capacity):
    flat_routes = routes.reshape(-1)
    onehot = (flat_routes[:, None] == jnp.arange(experts, dtype=jnp.int32)[None, :]).astype(jnp.int32)
    before = (jnp.cumsum(onehot, axis=0) - onehot).astype(jnp.int32)
    rank_pick = lax.optimization_barrier(jnp.sum(before * onehot, axis=1)).astype(jnp.int32)
    return (flat_routes * capacity + rank_pick).astype(jnp.int32)

def device_attention(query_rows, key_matrix, value_matrix, request_row, prompt_req, prompt_page_table, shared_prompt_cache):
    new_token_count = query_rows.shape[0]
    request_slot_count = prompt_req.shape[0]
    table = prompt_page_table.reshape(-1, PPP)
    page_indices = jnp.take(table, prompt_req, axis=0).reshape(-1)
    page_token_rows = jnp.take(shared_prompt_cache, page_indices, axis=0).reshape(request_slot_count * PROMPT_LENGTH, 2 * KEY_VALUE_HEADS, HEAD_WIDTH)
    every_key = jnp.concatenate([page_token_rows[:, :KEY_VALUE_HEADS], key_matrix], axis=0).astype(jnp.float32)
    every_value = jnp.concatenate([page_token_rows[:, KEY_VALUE_HEADS:], value_matrix], axis=0).astype(jnp.float32)
    token_index = jnp.arange(new_token_count, dtype=jnp.int32)
    owner_slot = jnp.arange(request_slot_count * PROMPT_LENGTH, dtype=jnp.int32) // PROMPT_LENGTH
    prompt_valid_mask = request_row[:, None] == owner_slot[None, :]
    local_ok = (request_row[:, None] == request_row[None, :]) & (token_index[None, :] <= token_index[:, None])
    allowed = jnp.concatenate([prompt_valid_mask, local_ok], axis=1)
    grouped_queries = query_rows.reshape(new_token_count, KEY_VALUE_HEADS, QUERY_HEADS // KEY_VALUE_HEADS, HEAD_WIDTH).astype(jnp.float32)
    scores = jnp.einsum('tkgd,nkd->tkgn', grouped_queries, every_key) * HEAD_WIDTH ** (-0.5)
    scores = jnp.where(allowed[:, None, None, :], scores, VERY_NEGATIVE)
    running_max = lax.optimization_barrier(jnp.max(scores, axis=-1, keepdims=True))
    weights = jnp.exp(scores - running_max)
    totals = lax.optimization_barrier(jnp.sum(weights, axis=-1))
    rounded = lax.optimization_barrier(weights.astype(jnp.bfloat16))
    summed = jnp.einsum('tkgn,nkd->tkgd', rounded.astype(jnp.float32), every_value)
    return (summed / totals[..., None]).reshape(new_token_count, QUERY_HEADS * HEAD_WIDTH).astype(jnp.bfloat16)

def reference(tokens, token_request_slot, request_prompt, request_adapter, prompt_page_table, shared_prompt_cache, routes, attention_norm_gain, query_matrix, key_value_weight, attention_output_weight, adapter_query_down, adapter_query_up, adapter_output_down, adapter_output_up, expert_norm_gain, router, expert_gate_up, expert_down):
    groups = token_request_slot.shape[0]
    new_token_count = token_request_slot.shape[1]
    request_slot_count = request_prompt.shape[0] // groups
    width = tokens.shape[1]

    def one_device(inputs):
        weight_matrix, request_row, prompt_req, adapter_req = inputs
        token_adapter, prompt_tok, token_positions = request_info(request_row, prompt_req, adapter_req)
        query_rows, key_matrix, value_matrix = apply_projection(weight_matrix, token_adapter, token_positions, attention_norm_gain, query_matrix, key_value_weight, adapter_query_down, adapter_query_up)
        attention_output = device_attention(query_rows, key_matrix, value_matrix, request_row, prompt_req, prompt_page_table, shared_prompt_cache)
        return finalize(attention_output, weight_matrix, token_adapter, attention_output_weight, adapter_output_down, adapter_output_up)
    hidden_state = lax.map(one_device, (tokens.reshape(groups, new_token_count, width), token_request_slot, request_prompt.reshape(groups, request_slot_count), request_adapter.reshape(groups, request_slot_count)))
    hidden_state = hidden_state.reshape(groups * new_token_count, width)
    ffn_normed = rms_norm(hidden_state, expert_norm_gain)
    gates = gate_weights(ffn_normed, router, routes)
    experts = expert_gate_up.shape[0]
    destination = jax.vmap(lambda block: slot_of(block, experts, CAP))(routes.reshape(groups, new_token_count, TOPK))
    normed_dev = ffn_normed.reshape(groups, new_token_count, width)
    gates_dev = gates.reshape(groups, new_token_count * TOPK)
    device_line = jnp.arange(groups, dtype=jnp.int32)[:, None]
    source = jnp.broadcast_to(jnp.arange(new_token_count * TOPK, dtype=jnp.int32) // TOPK, (groups, new_token_count * TOPK))

    def one_expert(totals, inputs):
        weight_in, weight_out, number = inputs
        routed = destination // CAP == number
        slot_index = jnp.where(routed, destination % CAP, CAP).astype(jnp.int32)
        token_of = jnp.zeros((groups, CAP + 1), jnp.int32).at[device_line, slot_index].set(source)[:, :CAP]
        gate_of = jnp.zeros((groups, CAP + 1), jnp.float32).at[device_line, slot_index].set(gates_dev)[:, :CAP]
        filled = jnp.zeros((groups, CAP + 1), jnp.bool_).at[device_line, slot_index].set(routed)[:, :CAP]
        chosen = jnp.where(filled[..., None], normed_dev[device_line, token_of], jnp.zeros((), jnp.bfloat16))
        inner = jnp.dot(chosen.reshape(groups * CAP, width), weight_in, preferred_element_type=jnp.float32)
        units = (jax.nn.relu(inner[:, :FFE]) * inner[:, FFE:]).astype(jnp.bfloat16)
        result = jnp.dot(units, weight_out, preferred_element_type=jnp.float32).astype(jnp.bfloat16)
        result = result.reshape(groups, CAP, width)
        added = jnp.where(filled[..., None], gate_of[..., None] * result.astype(jnp.float32), 0.0)
        totals = totals.at[device_line, token_of].add(added)
        return (totals, None)
    initial = jnp.zeros((groups, new_token_count, width), jnp.float32)
    totals, unused = lax.scan(one_expert, initial, (expert_gate_up, expert_down, jnp.arange(experts, dtype=jnp.int32)))
    mixed_rows = hidden_state.reshape(groups, new_token_count, width).astype(jnp.float32) + totals
    return mixed_rows.reshape(groups * new_token_count, width).astype(jnp.bfloat16)
```

```python
import jax
import jax.numpy as jnp
from jax import lax
from jax.experimental import pallas as pl
from jax.experimental.pallas import tpu as pltpu
from jax.sharding import PartitionSpec as P

MESH = pl.DeviceIdType.MESH
CAP = 48
FFE = 768

QUERY_HEADS = 12
KEY_VALUE_HEADS = 2
HEAD_WIDTH = 128
TOPK = 4
ADAPTER_RANK = 16
PPP = 16
PROMPT_LENGTH = 256


EPSILON = 1e-06
THETA = 1000000.0
VERY_NEGATIVE = -1e30


def rms_norm(weight_matrix, gain_vector):
    values = weight_matrix.astype(jnp.float32)
    factor = lax.rsqrt(jnp.mean(values * values, axis=-1, keepdims=True) + EPSILON)
    return (values * factor * gain_vector.astype(jnp.float32)).astype(jnp.bfloat16)


def apply_rotary(values, token_positions):
    half_width = values.shape[-1] // 2
    frequency = THETA ** (-jnp.arange(half_width).astype(jnp.float32) / half_width)
    angles = token_positions.astype(jnp.float32)[:, None] * frequency[None, :]
    cosine = jnp.cos(angles)[:, None, :]
    sine_table = jnp.sin(angles)[:, None, :]
    first_half = values[..., :half_width]
    second = values[..., half_width:]
    return jnp.concatenate(
        [first_half * cosine - second * sine_table, second * cosine + first_half * sine_table],
        axis=-1,
    )


def adapter_update(weight_matrix, down_proj, up_proj, token_adapter):
    inner = jnp.dot(weight_matrix, down_proj, preferred_element_type=jnp.float32)
    owner_slot = jnp.arange(down_proj.shape[1], dtype=jnp.int32) // ADAPTER_RANK
    inner = jnp.where(owner_slot[None, :] == token_adapter[:, None], inner, 0.0).astype(
        jnp.bfloat16
    )
    return jnp.dot(inner, up_proj, preferred_element_type=jnp.float32)


def request_info(request_row, prompt_req, adapter_req):
    new_token_count = request_row.shape[0]
    request_slot_count = prompt_req.shape[0]
    matches = request_row[:, None] == jnp.arange(request_slot_count, dtype=jnp.int32)[None, :]
    token_adapter = jnp.sum(jnp.where(matches, adapter_req[None, :], 0), axis=1)
    prompt_tok = jnp.sum(jnp.where(matches, prompt_req[None, :], 0), axis=1)
    token_index = jnp.arange(new_token_count, dtype=jnp.int32)
    first_row = jnp.min(jnp.where(matches, token_index[:, None], new_token_count), axis=0)
    start_tok = jnp.sum(jnp.where(matches, first_row[None, :], 0), axis=1)
    token_positions = PROMPT_LENGTH + token_index - start_tok
    return (token_adapter, prompt_tok, token_positions)


def apply_projection(
    tokens,
    token_adapter,
    token_positions,
    attention_norm_gain,
    query_matrix,
    key_value_weight,
    adapter_query_down,
    adapter_query_up,
):
    new_token_count = tokens.shape[0]
    normalized = rms_norm(tokens, attention_norm_gain)
    query_rows = jnp.dot(normalized, query_matrix, preferred_element_type=jnp.float32)
    query_rows = query_rows + adapter_update(
        normalized, adapter_query_down, adapter_query_up, token_adapter
    )
    query_rows = apply_rotary(
        query_rows.reshape(new_token_count, QUERY_HEADS, HEAD_WIDTH), token_positions
    ).astype(jnp.bfloat16)
    key_value_rows = jnp.dot(
        normalized, key_value_weight, preferred_element_type=jnp.float32
    ).reshape(new_token_count, 2 * KEY_VALUE_HEADS, HEAD_WIDTH)
    key_matrix = apply_rotary(key_value_rows[:, :KEY_VALUE_HEADS], token_positions).astype(
        jnp.bfloat16
    )
    value_matrix = key_value_rows[:, KEY_VALUE_HEADS:].astype(jnp.bfloat16)
    return (query_rows, key_matrix, value_matrix)


def finalize(
    attention_output,
    tokens,
    token_adapter,
    attention_output_weight,
    adapter_output_down,
    adapter_output_up,
):
    expert_mixture = jnp.dot(
        attention_output, attention_output_weight, preferred_element_type=jnp.float32
    )
    expert_mixture = expert_mixture + adapter_update(
        attention_output, adapter_output_down, adapter_output_up, token_adapter
    )
    return (tokens.astype(jnp.float32) + expert_mixture).astype(jnp.bfloat16)


def block_attention(running, grouped_queries, key_matrix, value_matrix, allowed):
    running_max, totals, accum = running
    scale = grouped_queries.shape[-1] ** (-0.5)
    scores = (
        jnp.einsum(
            "tkgd,nkd->tkgn", grouped_queries, key_matrix, preferred_element_type=jnp.float32
        )
        * scale
    )
    scores = jnp.where(allowed[:, None, None, :], scores, VERY_NEGATIVE)
    new_max = jnp.maximum(running_max, jnp.max(scores, axis=-1))
    factor = jnp.exp(running_max - new_max)
    weights = jnp.exp(scores - new_max[..., None])
    totals = totals * factor + jnp.sum(weights, axis=-1)
    summed = jnp.einsum(
        "tkgn,nkd->tkgd",
        weights.astype(jnp.bfloat16),
        value_matrix,
        preferred_element_type=jnp.float32,
    )
    accum = accum * factor[..., None] + summed
    return (new_max, totals, accum)


def moe_kernel(
    hid_ref, gain_ref, routes_ref, router_ref, wgu_ref, wdn_ref,
    out_ref,
    xbuf, rbuf, rank_s, gate_s, ct_s, pack, arrived, units, result, returned,
    psend, precv, acc,
    sa_x, ra_x, sa_r, ra_r, sb_p, rb_p, sb_r, rb_r, sp_s, sp_r,
):
    x = lax.axis_index("req")
    e_me = lax.axis_index("exp")
    y = e_me // 8
    z = lax.rem(e_me // 2, 4)
    c = lax.rem(e_me, 2)
    me_exp = e_me
    first_pos = y * (1 - c) + z * c
    first_base = z * 2 * (1 - c) + y * 8 * c + c
    first_step = 8 - 6 * c
    second_pos = z * (1 - c) + y * c
    second_base = y * 8 * (1 - c) + z * 2 * c
    second_step = 2 + 6 * c

    def first_dev(offset):
        return (x, first_base + lax.rem(first_pos + offset, 4) * first_step)

    def second_exp(offset, dc):
        return second_base + lax.rem(second_pos + offset, 4) * second_step + lax.rem(c + dc, 2)

    def relay_dev(j, dc):
        rc = lax.rem(c + dc, 2)
        pos = z * (1 - rc) + y * rc
        base = y * 8 * (1 - rc) + z * 2 * rc
        return (x, base + lax.rem(pos - j + 4, 4) * (2 + 6 * rc) + rc)

    def remote(src, dst, ssem, rsem, dev):
        return pltpu.make_async_remote_copy(
            src_ref=src, dst_ref=dst, send_sem=ssem, recv_sem=rsem,
            device_id=dev, device_id_type=MESH)

    barrier = pltpu.get_barrier_semaphore()
    for dy in range(4):
        for dc in range(2):
            if dy or dc:
                dev = (x, (lax.rem(y + dy, 4) * 4 + z) * 2 + lax.rem(c + dc, 2))
                pl.semaphore_signal(barrier, 1, device_id=dev, device_id_type=MESH)
    for dz in range(1, 4):
        for dc in range(2):
            dev = (x, (y * 4 + lax.rem(z + dz, 4)) * 2 + lax.rem(c + dc, 2))
            pl.semaphore_signal(barrier, 1, device_id=dev, device_id_type=MESH)

    hv = hid_ref[...].astype(jnp.float32)
    factor = lax.rsqrt(jnp.mean(hv * hv, axis=-1, keepdims=True) + EPSILON)
    xbuf[0] = (hv * factor * gain_ref[...].astype(jnp.float32)).astype(jnp.bfloat16)
    rbuf[0] = routes_ref[...]
    acc[...] = hv
    pl.semaphore_wait(barrier, 13)

    half = xbuf.shape[1] // 2
    x_copies = []
    for h in range(2):
        rows = pl.ds(h * half, half)
        for i, off in ((1, 1), (2, 3)):
            hh = h if i == 1 else 1 - h
            rows = pl.ds(hh * half, half)
            cp = remote(xbuf.at[0, rows], xbuf.at[i, rows], sa_x.at[i, hh], ra_x.at[i, hh], first_dev(off))
            cp.start()
            x_copies.append(cp)
    r_copies = []
    for i, off in ((1, 1), (2, 3), (3, 2)):
        cp = remote(rbuf.at[0], rbuf.at[i], sa_r.at[i], ra_r.at[i], first_dev(off))
        cp.start()
        r_copies.append(cp)

    tokens = xbuf.shape[1]
    row_i = lax.broadcasted_iota(jnp.int32, (tokens, tokens), 0)
    col_i = lax.broadcasted_iota(jnp.int32, (tokens, tokens), 1)
    before = jnp.where(row_i < col_i, 1.0, 0.0).astype(jnp.bfloat16)
    experts = router_ref.shape[0]
    width = xbuf.shape[2]

    def make_tables(i):
        r = rbuf[i]
        ei = lax.broadcasted_iota(jnp.int32, (experts, tokens), 0)
        hit = ei == r[0:1, :]
        for k in range(1, TOPK):
            hit = jnp.logical_or(hit, ei == r[k:k + 1, :])
        hit_f = jnp.where(hit, 1.0, 0.0)
        rank = jnp.dot(hit_f.astype(jnp.bfloat16), before, preferred_element_type=jnp.float32)
        rank_s[i] = jnp.where(hit, rank, -1.0)
        logits = lax.dot_general(router_ref[...], xbuf[i], (((1,), (1,)), ((), ())),
                                 preferred_element_type=jnp.float32)
        sig = jnp.where(hit, jax.nn.sigmoid(logits), 0.0)
        gate_s[i] = sig / jnp.sum(sig, axis=0, keepdims=True)

    slot_i = lax.broadcasted_iota(jnp.int32, (CAP, tokens), 0).astype(jnp.float32)
    tile = 512

    def dispatch(i):
        picks = []
        for j in range(4):
            for dc in range(2):
                e = second_exp(j, dc)
                rank_row = rank_s[i, pl.ds(e, 1), :]
                gate_row = gate_s[i, pl.ds(e, 1), :]
                eq = slot_i == rank_row
                picks.append(jnp.where(eq, 1.0, 0.0).astype(jnp.bfloat16))
                q = j * 2 + dc
                ct_s[i, q * CAP:(q + 1) * CAP, :] = jnp.where(eq, gate_row, 0.0).astype(jnp.bfloat16)
        pick = jnp.concatenate(picks, axis=0)

        @pl.loop(0, width // tile)
        def _(n):
            cols = pl.ds(pl.multiple_of(n * tile, tile), tile)
            rows = jnp.dot(pick, xbuf[i, :, cols], preferred_element_type=jnp.float32).astype(jnp.bfloat16)
            arrived[i, 0:CAP, cols] = rows[0:CAP]
            pack[i, :, cols] = rows
        for q in range(1, 8):
            pack_copy(i, q).start()

    def pack_copy(i, q):
        j, dc = q // 2, q % 2
        return remote(pack.at[i, pl.ds(q * CAP, CAP)], arrived.at[i, pl.ds(q * CAP, CAP)],
                      sb_p.at[i, q], rb_p.at[i, q], (x, second_exp(j, dc)))

    def result_copy(i, q):
        j, dc = q // 2, q % 2
        return remote(result.at[i, pl.ds(q * CAP, CAP)], returned.at[i, pl.ds(q * CAP, CAP)],
                      sb_r.at[i, q], rb_r.at[i, q], relay_dev(j, dc))

    def expert(i):
        for q in range(1, 8):
            pack_copy(i, q).wait_recv()

        @pl.loop(0, FFE // 256)
        def _(n):
            up_cols = pl.ds(pl.multiple_of(FFE + n * 256, 256), 256)
            cols = pl.ds(pl.multiple_of(n * 256, 256), 256)
            a = arrived[i]
            g = jnp.dot(a, wgu_ref[:, cols], preferred_element_type=jnp.float32)
            u = jnp.dot(a, wgu_ref[:, up_cols], preferred_element_type=jnp.float32)
            units[:, cols] = (jnp.maximum(g, 0.0) * u).astype(jnp.bfloat16)

        @pl.loop(0, width // tile)
        def _(n):
            cols = pl.ds(pl.multiple_of(n * tile, tile), tile)
            rows = jnp.dot(units[...], wdn_ref[:, cols], preferred_element_type=jnp.float32).astype(jnp.bfloat16)
            returned[i, 0:CAP, cols] = rows[0:CAP]
            result[i, :, cols] = rows
        for q in range(1, 8):
            result_copy(i, q).start()

    offsets = (0, 1, 3, 2)

    def partial_copy(i):
        return remote(psend.at[i - 1], precv.at[i - 1], sp_s.at[i - 1], sp_r.at[i - 1],
                      first_dev(4 - offsets[i]))

    def combine(i):
        for q in range(1, 8):
            result_copy(i, q).wait_recv()

        @pl.loop(0, width // tile)
        def _(n):
            cols = pl.ds(pl.multiple_of(n * tile, tile), tile)
            part = lax.dot_general(ct_s[i], returned[i, :, cols], (((0,), (0,)), ((), ())),
                                   preferred_element_type=jnp.float32)
            if i == 0:
                acc[:, cols] = acc[:, cols] + part
            else:
                psend[i - 1, :, cols] = part.astype(jnp.bfloat16)
        if i:
            partial_copy(i).start()

    def forward(i):
        h = 0 if i == 1 else 1
        rows = pl.ds(h * half, half)
        return remote(xbuf.at[i, rows], xbuf.at[3, rows], sa_x.at[3, h], ra_x.at[3, h],
                      first_dev(1 if i == 1 else 3))

    make_tables(0)
    dispatch(0)
    x_copies[0].wait_recv()
    forward(1).start()
    x_copies[1].wait_recv()
    forward(2).start()
    for i in (1, 2, 3):
        r_copies[i - 1].wait_recv()
        if i == 3:
            forward(1).wait_recv()
            forward(2).wait_recv()
        else:
            x_copies[2 + i - 1].wait_recv()
        make_tables(i)
        dispatch(i)
        expert(i - 1)
        if i >= 2:
            combine(i - 2)
    expert(3)
    combine(2)
    combine(3)
    for i in (1, 2, 3):
        partial_copy(i).wait_recv()
    out_ref[...] = (acc[...] + precv[0].astype(jnp.float32) + precv[1].astype(jnp.float32)
                    + precv[2].astype(jnp.float32)).astype(jnp.bfloat16)
    for cp in x_copies + r_copies:
        cp.wait_send()
    forward(1).wait_send()
    forward(2).wait_send()
    for i in range(4):
        for q in range(1, 8):
            pack_copy(i, q).wait_send()
            result_copy(i, q).wait_send()
        if i:
            partial_copy(i).wait_send()


def moe(hidden, expert_norm_gain, routes, router, expert_gate_up, expert_down):
    tokens, width = hidden.shape
    experts = router.shape[1]
    routes_t = jnp.concatenate(
        [routes.T, jnp.full((8 - TOPK, tokens), -1, jnp.int32)], axis=0)
    bf, f32 = jnp.bfloat16, jnp.float32
    rows = 8 * CAP
    dma = pltpu.SemaphoreType.DMA
    return pl.pallas_call(
        moe_kernel,
        out_shape=jax.ShapeDtypeStruct((tokens, width), bf),
        in_specs=[pl.BlockSpec(memory_space=pltpu.VMEM)] * 6,
        out_specs=pl.BlockSpec(memory_space=pltpu.VMEM),
        scratch_shapes=[
            pltpu.VMEM((4, tokens, width), bf),
            pltpu.VMEM((4, 8, tokens), jnp.int32),
            pltpu.VMEM((4, experts, tokens), f32),
            pltpu.VMEM((4, experts, tokens), f32),
            pltpu.VMEM((4, rows, tokens), bf),
            pltpu.VMEM((4, rows, width), bf),
            pltpu.VMEM((4, rows, width), bf),
            pltpu.VMEM((rows, FFE), bf),
            pltpu.VMEM((4, rows, width), bf),
            pltpu.VMEM((4, rows, width), bf),
            pltpu.VMEM((3, tokens, width), bf),
            pltpu.VMEM((3, tokens, width), bf),
            pltpu.VMEM((tokens, width), f32),
            dma((4, 2)), dma((4, 2)), dma((4,)), dma((4,)),
            dma((4, 8)), dma((4, 8)), dma((4, 8)), dma((4, 8)),
            dma((3,)), dma((3,)),
        ],
        compiler_params=pltpu.CompilerParams(
            collective_id=1, has_side_effects=True, vmem_limit_bytes=60 * 1024 * 1024),
        name="moe",
    )(hidden, expert_norm_gain.reshape(1, width), routes_t, router.T,
      expert_gate_up.reshape(expert_gate_up.shape[-2:]), expert_down.reshape(expert_down.shape[-2:]))


def on_device(
    tokens,
    token_request_slot,
    request_prompt,
    request_adapter,
    prompt_page_table,
    shared_prompt_cache,
    routes,
    attention_norm_gain,
    query_matrix,
    key_value_weight,
    attention_output_weight,
    adapter_query_down,
    adapter_query_up,
    adapter_output_down,
    adapter_output_up,
    expert_norm_gain,
    router,
    expert_gate_up,
    expert_down,
):
    new_token_count = tokens.shape[0]
    request_row = token_request_slot[0]
    request_slot_count = request_prompt.shape[0]
    token_adapter, prompt_tok, token_positions = request_info(
        request_row, request_prompt, request_adapter
    )
    query_rows, key_matrix, value_matrix = apply_projection(
        tokens,
        token_adapter,
        token_positions,
        attention_norm_gain,
        query_matrix,
        key_value_weight,
        adapter_query_down,
        adapter_query_up,
    )
    query_group_width = QUERY_HEADS // KEY_VALUE_HEADS
    grouped_queries = query_rows.reshape(
        new_token_count, KEY_VALUE_HEADS, query_group_width, HEAD_WIDTH
    )
    token_index = jnp.arange(new_token_count, dtype=jnp.int32)
    local_ok = (request_row[:, None] == request_row[None, :]) & (
        token_index[None, :] <= token_index[:, None]
    )
    initial = (
        jnp.full((new_token_count, KEY_VALUE_HEADS, query_group_width), VERY_NEGATIVE, jnp.float32),
        jnp.zeros((new_token_count, KEY_VALUE_HEADS, query_group_width), jnp.float32),
        jnp.zeros((new_token_count, KEY_VALUE_HEADS, query_group_width, HEAD_WIDTH), jnp.float32),
    )
    running_progress = block_attention(initial, grouped_queries, key_matrix, value_matrix, local_ok)
    requested_pages = jnp.take(prompt_page_table.reshape(-1, PPP), request_prompt, axis=0).reshape(
        -1
    )
    complete_cache = lax.all_gather(shared_prompt_cache, ("req", "exp"), axis=0, tiled=True)
    page_token_rows = jnp.take(complete_cache, requested_pages, axis=0).reshape(
        request_slot_count * PROMPT_LENGTH, 2 * KEY_VALUE_HEADS, HEAD_WIDTH
    )
    owner_slot = jnp.arange(request_slot_count * PROMPT_LENGTH, dtype=jnp.int32) // PROMPT_LENGTH
    prompt_valid_mask = request_row[:, None] == owner_slot[None, :]
    running_progress = block_attention(
        running_progress,
        grouped_queries,
        page_token_rows[:, :KEY_VALUE_HEADS],
        page_token_rows[:, KEY_VALUE_HEADS:],
        prompt_valid_mask,
    )
    running_max, totals, accum = running_progress
    attention_output = (
        (accum / totals[..., None])
        .reshape(new_token_count, QUERY_HEADS * HEAD_WIDTH)
        .astype(jnp.bfloat16)
    )
    hidden_state = finalize(
        attention_output,
        tokens,
        token_adapter,
        attention_output_weight,
        adapter_output_down,
        adapter_output_up,
    )
    return moe(hidden_state, expert_norm_gain, routes, router, expert_gate_up, expert_down)


def solution(mesh):
    return jax.shard_map(
        on_device,
        mesh=mesh,
        in_specs=(
            P(("req", "exp"), None),
            P(("req", "exp"), None),
            P(("req", "exp")),
            P(("req", "exp")),
            P(),
            P(("req", "exp"), None, None),
            P(("req", "exp"), None),
            P(),
            P(),
            P(),
            P(),
            P(),
            P(),
            P(),
            P(),
            P(),
            P(),
            P("exp", None, None),
            P("exp", None, None),
        ),
        out_specs=P(("req", "exp"), None),
        check_vma=False,
    )
```

```python
import math

import jax
import jax.numpy as jnp
from jax import lax
from jax.experimental import pallas as pl
from jax.experimental.pallas import tpu as pltpu
from jax.sharding import PartitionSpec as P

MESH = pl.DeviceIdType.MESH
CAP = 48
FFE = 768

QUERY_HEADS = 12
KEY_VALUE_HEADS = 2
HEAD_WIDTH = 128
TOPK = 4
ADAPTER_RANK = 16
PPP = 16
PROMPT_LENGTH = 256


EPSILON = 1e-06
THETA = 1000000.0
VERY_NEGATIVE = -1e30


TILE_GROUPS = ((0, 6), (6, 5), (11, 5))
AXIS_ORDERS = ((0, 1, 2), (1, 2, 0), (2, 0, 1))


def front_kernel(
    slot_ref, prompt_ref, adapter_ref, table_ref, tokens_ref, cache_ref, gain_ref,
    wq_any, wkv_any, aqd_any, aqu_any, wo_any, aod_any, aou_any,
    hid_ref,
    cache, wq, wkv, aqd, aqu, wo, aod, aou,
    normed, inner_s, cos_s, sin_s, q_s, k_s, v_s, kv_s, att,
    w_sem, c_sem, ag_s, ag_r, co_s, co_r,
):
    x = lax.axis_index("req")
    e_me = lax.axis_index("exp")
    y = e_me // 8
    z = lax.rem(e_me // 2, 4)
    c = lax.rem(e_me, 2)
    here = (x, y, z)

    def device(axis, offset):
        p = list(here)
        p[axis] = lax.rem(p[axis] + offset, 4)
        return (p[0], (p[1] * 4 + p[2]) * 2 + c)

    partner = (x, (y * 4 + z) * 2 + 1 - c)

    barrier = pltpu.get_barrier_semaphore()
    for axis in range(3):
        for off in (1, 3):
            pl.semaphore_signal(barrier, 1, device_id=device(axis, off), device_id_type=MESH)
    pl.semaphore_signal(barrier, 1, device_id=partner, device_id_type=MESH)

    own = []
    for p in range(4):
        for col in range(4):
            cp = pltpu.make_async_copy(
                cache_ref.at[p, :, pl.ds(col * 128, 128)],
                cache.at[x, y, z, c, p * 4 + col], c_sem.at[p * 4 + col])
            cp.start()
            own.append(cp)
    weights = []
    for i, (src, dst) in enumerate((
            (wkv_any, wkv), (aqd_any, aqd), (aqu_any, aqu), (wq_any, wq),
            (aod_any, aod), (wo_any, wo), (aou_any, aou))):
        cp = pltpu.make_async_copy(src, dst, w_sem.at[i])
        cp.start()
        weights.append(cp)

    def block(where, first, count):
        return cache.at[where[0], where[1], where[2], c, pl.ds(first, count)]

    def step(g, phase, kind, axis, where):
        lo, n = TILE_GROUPS[g]
        if kind == 2:
            n = n // 2
        elif kind == 3:
            lo, n = lo + n // 2, n - n // 2
        view = block(where, lo, n)
        return pltpu.make_async_remote_copy(
            src_ref=view, dst_ref=view, send_sem=ag_s.at[g, phase, kind], recv_sem=ag_r.at[g, phase, kind],
            device_id=device(axis, 1 if kind in (0, 2) else 3), device_id_type=MESH)

    every = slice(None)

    def place(g, second, third):
        order = AXIS_ORDERS[g]
        w = [every, every, every]
        for axis, off in ((order[1], second), (order[2], third)):
            if off is not None:
                w[axis] = lax.rem(here[axis] + off, 4)
        return w

    class Ring:
        def __init__(self, g, phase, axis, where_of):
            self.g, self.phase, self.axis, self.where_of = g, phase, axis, where_of

        def cp(self, kind, off):
            return step(self.g, self.phase, kind, self.axis, self.where_of(off))

        def begin(self):
            self.cp(0, 0).start()
            self.cp(1, 0).start()

        def pass_on(self):
            self.cp(0, 3).wait_recv()
            self.cp(2, 3).start()
            self.cp(1, 1).wait_recv()
            self.cp(3, 1).start()

        def finish(self):
            self.cp(2, 2).wait_recv()
            self.cp(3, 2).wait_recv()

        def drain(self):
            self.cp(0, 0).wait_send()
            self.cp(1, 0).wait_send()
            self.cp(2, 3).wait_send()
            self.cp(3, 1).wait_send()

    def first_where(g):
        def f(off):
            order = AXIS_ORDERS[g]
            w = [here[0], here[1], here[2]]
            w[order[0]] = lax.rem(here[order[0]] + off, 4)
            return w
        return f

    groups = range(3)
    ring1 = [Ring(g, 0, AXIS_ORDERS[g][0], first_where(g)) for g in groups]
    ring2 = [Ring(g, 1, AXIS_ORDERS[g][1], lambda off, g=g: place(g, off, 0)) for g in groups]
    ring3 = [[Ring(g, 2 + o, AXIS_ORDERS[g][2], lambda off, g=g, o=o: place(g, o, off)) for o in range(4)]
             for g in groups]

    def share(g, i, second, third):
        lo, n = TILE_GROUPS[g]
        view = block(place(g, second, third), lo, n)
        return pltpu.make_async_remote_copy(
            src_ref=view, dst_ref=view, send_sem=co_s.at[g, i], recv_sem=co_r.at[g, i],
            device_id=partner, device_id_type=MESH)

    def share_mine(g, i):
        if i == 0:
            return share(g, 0, None, 0)
        return share(g, i, (i - 1) // 3, 1 + (i - 1) % 3)

    def theirs(g, i):
        lo, n = TILE_GROUPS[g]
        second, third = (None, 0) if i == 0 else ((i - 1) // 3, 1 + (i - 1) % 3)
        w = place(g, second, third)
        view = cache.at[w[0], w[1], w[2], 1 - c, pl.ds(lo, n)]
        return pltpu.make_async_remote_copy(
            src_ref=view, dst_ref=view, send_sem=co_s.at[g, i], recv_sem=co_r.at[g, i],
            device_id=partner, device_id_type=MESH)

    tokens = tokens_ref.shape[0]
    width = tokens_ref.shape[1]
    half_rows = tokens // 2

    for cp in own:
        cp.wait()
    pl.semaphore_wait(barrier, 7)
    for g in groups:
        ring1[g].begin()

    tv = tokens_ref[...].astype(jnp.float32)
    factor = lax.rsqrt(jnp.mean(tv * tv, axis=-1, keepdims=True) + EPSILON)
    normed[...] = (tv * factor * gain_ref[...].astype(jnp.float32)).astype(jnp.bfloat16)

    slot_row = slot_ref[...]
    index_col = lax.broadcasted_iota(jnp.int32, (tokens, 1), 0).astype(jnp.float32)
    slot_col = jnp.zeros((tokens, 1), jnp.float32)
    start_col = jnp.zeros((tokens, 1), jnp.float32)
    adapter_col = jnp.zeros((tokens, 1), jnp.int32) + adapter_ref[0]
    for r in range(1, 4):
        start = jnp.sum(jnp.where(slot_row < r, 1.0, 0.0), axis=1, keepdims=True)
        reached = index_col >= start
        slot_col = jnp.where(reached, float(r), slot_col)
        start_col = jnp.where(reached, start, start_col)
        adapter_col = jnp.where(reached, adapter_ref[r], adapter_col)
    position = index_col - start_col + float(PROMPT_LENGTH)
    lane = lax.broadcasted_iota(jnp.int32, (1, HEAD_WIDTH), 1)
    pair = lax.rem(lane, HEAD_WIDTH // 2).astype(jnp.float32)
    frequency = jnp.exp(pair * (-math.log(THETA) / (HEAD_WIDTH // 2)))
    angle = position * frequency
    cos_s[...] = jnp.cos(angle)
    sin_s[...] = jnp.where(lane < HEAD_WIDTH // 2, -jnp.sin(angle), jnp.sin(angle))

    def rotate(v):
        return v * cos_s[...] + pltpu.roll(v, HEAD_WIDTH // 2, 1) * sin_s[...]

    for g in groups:
        ring1[g].pass_on()

    weights[0].wait()
    kv = jnp.dot(normed[...], wkv[...], preferred_element_type=jnp.float32)
    for h in range(2):
        k_s[h] = rotate(kv[:, h * 128:(h + 1) * 128]).astype(jnp.bfloat16)
        v_s[h] = kv[:, 256 + h * 128:256 + (h + 1) * 128].astype(jnp.bfloat16)

    for g in groups:
        ring1[g].finish()
        ring2[g].begin()
        ring3[g][0].begin()

    owner = lax.broadcasted_iota(jnp.int32, (tokens, aqd.shape[1]), 1) // ADAPTER_RANK
    mine = owner == adapter_col
    weights[1].wait()
    inner = jnp.dot(normed[...], aqd[...], preferred_element_type=jnp.float32)
    inner_s[...] = jnp.where(mine, inner, 0.0).astype(jnp.bfloat16)
    weights[2].wait()
    weights[3].wait()

    def queries(lo, hi):
        @pl.loop(lo, hi)
        def _(n):
            cols = pl.ds(pl.multiple_of(n * 256, 256), 256)
            qv = jnp.dot(normed[...], wq[:, cols], preferred_element_type=jnp.float32)
            qv = qv + jnp.dot(inner_s[...], aqu[:, cols], preferred_element_type=jnp.float32)
            for h in range(2):
                q_s[n * 2 + h] = rotate(qv[:, h * 128:(h + 1) * 128]).astype(jnp.bfloat16)

    queries(0, 3)
    for g in groups:
        ring2[g].pass_on()
        ring3[g][3].begin()
        ring3[g][1].begin()
    queries(3, 6)
    for g in groups:
        ring3[g][0].pass_on()
        ring2[g].finish()
        ring3[g][2].begin()
        share_mine(g, 0).start()
    for o, before in ((3, 0), (1, 3), (2, 1)):
        for g in groups:
            ring3[g][o].pass_on()
            ring3[g][before].finish()
            for third in range(3):
                share_mine(g, 1 + before * 3 + third).start()
    for g in groups:
        ring3[g][2].finish()
        for third in range(3):
            share_mine(g, 1 + 2 * 3 + third).start()
    for g in groups:
        for i in range(13):
            theirs(g, i).wait_recv()

    @pl.loop(0, 4)
    def _(r):
        base = prompt_ref[r] * PPP
        for j in range(PPP):
            page = table_ref[base + j]
            d = page // 4
            px, py, pz, pc = d // 32, lax.rem(d // 8, 4), lax.rem(d // 2, 4), lax.rem(d, 2)
            t = lax.rem(page, 4) * 4
            for col in range(4):
                kv_s[col, r, pl.ds(j * 16, 16), :] = cache[px, py, pz, pc, t + col]

    scale = HEAD_WIDTH ** (-0.5)
    group = QUERY_HEADS // KEY_VALUE_HEADS
    nt = (((1,), (1,)), ((), ()))

    @pl.loop(0, KEY_VALUE_HEADS)
    def _(h):
        for b in range(2):
            rows = slice(b * half_rows, (b + 1) * half_rows)
            keys = (b + 1) * half_rows
            q = q_s[pl.ds(h * group, group), rows, :].reshape(group * half_rows, HEAD_WIDTH)
            slot = slot_col[rows]
            ki = lax.broadcasted_iota(jnp.int32, (half_rows, keys), 1).astype(jnp.float32)
            ok = jnp.logical_and(ki <= index_col[rows], ki >= start_col[rows])
            local = lax.dot_general(q, k_s[h, 0:keys], nt, preferred_element_type=jnp.float32)
            local = local.reshape(group, half_rows, keys) * scale
            local = jnp.where(ok[None], local, VERY_NEGATIVE)
            picked = None
            for r in range(b, b + 3):
                s = lax.dot_general(q, kv_s[h, r], nt, preferred_element_type=jnp.float32)
                s = s.reshape(group, half_rows, PROMPT_LENGTH)
                picked = s if picked is None else jnp.where((slot == float(r))[None], s, picked)
            picked = picked * scale
            top = jnp.maximum(jnp.max(picked, axis=-1, keepdims=True), jnp.max(local, axis=-1, keepdims=True))
            wp = jnp.exp(picked - top)
            wl = jnp.exp(local - top)
            total = jnp.sum(wp, axis=-1, keepdims=True) + jnp.sum(wl, axis=-1, keepdims=True)
            wp = wp.astype(jnp.bfloat16).reshape(group * half_rows, PROMPT_LENGTH)
            wl = wl.astype(jnp.bfloat16).reshape(group * half_rows, keys)
            summed = None
            for r in range(b, b + 3):
                o = jnp.dot(wp, kv_s[KEY_VALUE_HEADS + h, r], preferred_element_type=jnp.float32)
                o = o.reshape(group, half_rows, HEAD_WIDTH)
                summed = o if summed is None else jnp.where((slot == float(r))[None], o, summed)
            o = jnp.dot(wl, v_s[h, 0:keys], preferred_element_type=jnp.float32)
            summed = (summed + o.reshape(group, half_rows, HEAD_WIDTH)) / total
            for i in range(group):
                col = pl.multiple_of((h * group + i) * HEAD_WIDTH, HEAD_WIDTH)
                att[rows, pl.ds(col, HEAD_WIDTH)] = summed[i].astype(jnp.bfloat16)

    for cp in weights[4:]:
        cp.wait()
    inner = jnp.dot(att[...], aod[...], preferred_element_type=jnp.float32)
    inner_s[...] = jnp.where(mine, inner, 0.0).astype(jnp.bfloat16)

    @pl.loop(0, width // 512)
    def _(n):
        cols = pl.ds(pl.multiple_of(n * 512, 512), 512)
        mix = jnp.dot(att[...], wo[:, cols], preferred_element_type=jnp.float32)
        mix = mix + jnp.dot(inner_s[...], aou[:, cols], preferred_element_type=jnp.float32)
        hid_ref[:, cols] = (tokens_ref[:, cols].astype(jnp.float32) + mix).astype(jnp.bfloat16)

    for g in groups:
        ring1[g].drain()
        ring2[g].drain()
        for o in range(4):
            ring3[g][o].drain()
        for i in range(13):
            share_mine(g, i).wait_send()


def front(slots, prompts, adapters, table, tokens, shard, gain, wq, wkv, wo, aqd, aqu, aod, aou):
    rows, width = tokens.shape
    bf, f32 = jnp.bfloat16, jnp.float32
    dma = pltpu.SemaphoreType.DMA
    vmem = pl.BlockSpec(memory_space=pltpu.VMEM)
    smem = pl.BlockSpec(memory_space=pltpu.SMEM)
    hbm = pl.BlockSpec(memory_space=pl.ANY)
    ordered = (wq, wkv, aqd, aqu, wo, aod, aou)
    return pl.pallas_call(
        front_kernel,
        out_shape=jax.ShapeDtypeStruct((rows, width), bf),
        in_specs=[vmem, smem, smem, smem, vmem, hbm, vmem] + [hbm] * 7,
        out_specs=vmem,
        scratch_shapes=[pltpu.VMEM((4, 4, 4, 2, 16, 16, 128), bf)]
        + [pltpu.VMEM(w.shape, bf) for w in ordered]
        + [
            pltpu.VMEM((rows, width), bf),
            pltpu.VMEM((rows, aqd.shape[1]), bf),
            pltpu.VMEM((rows, HEAD_WIDTH), f32),
            pltpu.VMEM((rows, HEAD_WIDTH), f32),
            pltpu.VMEM((QUERY_HEADS, rows, HEAD_WIDTH), bf),
            pltpu.VMEM((KEY_VALUE_HEADS, rows, HEAD_WIDTH), bf),
            pltpu.VMEM((KEY_VALUE_HEADS, rows, HEAD_WIDTH), bf),
            pltpu.VMEM((2 * KEY_VALUE_HEADS, 4, PROMPT_LENGTH, HEAD_WIDTH), bf),
            pltpu.VMEM((rows, width), bf),
            dma((7,)), dma((16,)), dma((3, 6, 4)), dma((3, 6, 4)), dma((3, 13)), dma((3, 13)),
        ],
        compiler_params=pltpu.CompilerParams(
            collective_id=2, has_side_effects=True, vmem_limit_bytes=60 * 1024 * 1024),
        name="front",
    )(slots, prompts, adapters, table, tokens, shard, gain.reshape(1, width), *ordered)


def moe_kernel(
    hid_ref, gain_ref, routes_ref, router_ref, wgu_ref, wdn_ref,
    out_ref,
    xbuf, rbuf, rank_s, gate_s, ct_s, pack, arrived, units, result, returned,
    psend, precv, acc,
    sa_x, ra_x, sa_r, ra_r, sb_p, rb_p, sb_r, rb_r, sp_s, sp_r,
):
    x = lax.axis_index("req")
    e_me = lax.axis_index("exp")
    y = e_me // 8
    z = lax.rem(e_me // 2, 4)
    c = lax.rem(e_me, 2)
    me_exp = e_me
    first_pos = y * (1 - c) + z * c
    first_base = z * 2 * (1 - c) + y * 8 * c + c
    first_step = 8 - 6 * c
    second_pos = z * (1 - c) + y * c
    second_base = y * 8 * (1 - c) + z * 2 * c
    second_step = 2 + 6 * c

    def first_dev(offset):
        return (x, first_base + lax.rem(first_pos + offset, 4) * first_step)

    def second_exp(offset, dc):
        return second_base + lax.rem(second_pos + offset, 4) * second_step + lax.rem(c + dc, 2)

    def relay_dev(j, dc):
        rc = lax.rem(c + dc, 2)
        pos = z * (1 - rc) + y * rc
        base = y * 8 * (1 - rc) + z * 2 * rc
        return (x, base + lax.rem(pos - j + 4, 4) * (2 + 6 * rc) + rc)

    def remote(src, dst, ssem, rsem, dev):
        return pltpu.make_async_remote_copy(
            src_ref=src, dst_ref=dst, send_sem=ssem, recv_sem=rsem,
            device_id=dev, device_id_type=MESH)

    barrier = pltpu.get_barrier_semaphore()
    for dy in range(4):
        for dc in range(2):
            if dy or dc:
                dev = (x, (lax.rem(y + dy, 4) * 4 + z) * 2 + lax.rem(c + dc, 2))
                pl.semaphore_signal(barrier, 1, device_id=dev, device_id_type=MESH)
    for dz in range(1, 4):
        for dc in range(2):
            dev = (x, (y * 4 + lax.rem(z + dz, 4)) * 2 + lax.rem(c + dc, 2))
            pl.semaphore_signal(barrier, 1, device_id=dev, device_id_type=MESH)

    hv = hid_ref[...].astype(jnp.float32)
    factor = lax.rsqrt(jnp.mean(hv * hv, axis=-1, keepdims=True) + EPSILON)
    xbuf[0] = (hv * factor * gain_ref[...].astype(jnp.float32)).astype(jnp.bfloat16)
    rbuf[0] = routes_ref[...]
    acc[...] = hv
    pl.semaphore_wait(barrier, 13)

    half = xbuf.shape[1] // 2
    x_copies = []
    for h in range(2):
        rows = pl.ds(h * half, half)
        for i, off in ((1, 1), (2, 3)):
            hh = h if i == 1 else 1 - h
            rows = pl.ds(hh * half, half)
            cp = remote(xbuf.at[0, rows], xbuf.at[i, rows], sa_x.at[i, hh], ra_x.at[i, hh], first_dev(off))
            cp.start()
            x_copies.append(cp)
    r_copies = []
    for i, off in ((1, 1), (2, 3), (3, 2)):
        cp = remote(rbuf.at[0], rbuf.at[i], sa_r.at[i], ra_r.at[i], first_dev(off))
        cp.start()
        r_copies.append(cp)

    tokens = xbuf.shape[1]
    row_i = lax.broadcasted_iota(jnp.int32, (tokens, tokens), 0)
    col_i = lax.broadcasted_iota(jnp.int32, (tokens, tokens), 1)
    before = jnp.where(row_i < col_i, 1.0, 0.0).astype(jnp.bfloat16)
    experts = router_ref.shape[0]
    width = xbuf.shape[2]

    def make_tables(i):
        r = rbuf[i]
        ei = lax.broadcasted_iota(jnp.int32, (experts, tokens), 0)
        hit = ei == r[0:1, :]
        for k in range(1, TOPK):
            hit = jnp.logical_or(hit, ei == r[k:k + 1, :])
        hit_f = jnp.where(hit, 1.0, 0.0)
        rank = jnp.dot(hit_f.astype(jnp.bfloat16), before, preferred_element_type=jnp.float32)
        rank_s[i] = jnp.where(hit, rank, -1.0)
        logits = lax.dot_general(router_ref[...], xbuf[i], (((1,), (1,)), ((), ())),
                                 preferred_element_type=jnp.float32)
        sig = jnp.where(hit, jax.nn.sigmoid(logits), 0.0)
        gate_s[i] = sig / jnp.sum(sig, axis=0, keepdims=True)

    slot_i = lax.broadcasted_iota(jnp.int32, (CAP, tokens), 0).astype(jnp.float32)
    tile = 512

    def dispatch(i):
        picks = []
        for j in range(4):
            for dc in range(2):
                e = second_exp(j, dc)
                rank_row = rank_s[i, pl.ds(e, 1), :]
                gate_row = gate_s[i, pl.ds(e, 1), :]
                eq = slot_i == rank_row
                picks.append(jnp.where(eq, 1.0, 0.0).astype(jnp.bfloat16))
                q = j * 2 + dc
                ct_s[i, q * CAP:(q + 1) * CAP, :] = jnp.where(eq, gate_row, 0.0).astype(jnp.bfloat16)
        pick = jnp.concatenate(picks, axis=0)

        @pl.loop(0, width // tile)
        def _(n):
            cols = pl.ds(pl.multiple_of(n * tile, tile), tile)
            rows = jnp.dot(pick, xbuf[i, :, cols], preferred_element_type=jnp.float32).astype(jnp.bfloat16)
            arrived[i, 0:CAP, cols] = rows[0:CAP]
            pack[i, :, cols] = rows
        for q in range(1, 8):
            pack_copy(i, q).start()

    def pack_copy(i, q):
        j, dc = q // 2, q % 2
        return remote(pack.at[i, pl.ds(q * CAP, CAP)], arrived.at[i, pl.ds(q * CAP, CAP)],
                      sb_p.at[i, q], rb_p.at[i, q], (x, second_exp(j, dc)))

    def result_copy(i, q):
        j, dc = q // 2, q % 2
        return remote(result.at[i, pl.ds(q * CAP, CAP)], returned.at[i, pl.ds(q * CAP, CAP)],
                      sb_r.at[i, q], rb_r.at[i, q], relay_dev(j, dc))

    def expert(i):
        for q in range(1, 8):
            pack_copy(i, q).wait_recv()

        @pl.loop(0, FFE // 256)
        def _(n):
            up_cols = pl.ds(pl.multiple_of(FFE + n * 256, 256), 256)
            cols = pl.ds(pl.multiple_of(n * 256, 256), 256)
            a = arrived[i]
            g = jnp.dot(a, wgu_ref[:, cols], preferred_element_type=jnp.float32)
            u = jnp.dot(a, wgu_ref[:, up_cols], preferred_element_type=jnp.float32)
            units[:, cols] = (jnp.maximum(g, 0.0) * u).astype(jnp.bfloat16)

        @pl.loop(0, width // tile)
        def _(n):
            cols = pl.ds(pl.multiple_of(n * tile, tile), tile)
            rows = jnp.dot(units[...], wdn_ref[:, cols], preferred_element_type=jnp.float32).astype(jnp.bfloat16)
            returned[i, 0:CAP, cols] = rows[0:CAP]
            result[i, :, cols] = rows
        for q in range(1, 8):
            result_copy(i, q).start()

    offsets = (0, 1, 3, 2)

    def partial_copy(i):
        return remote(psend.at[i - 1], precv.at[i - 1], sp_s.at[i - 1], sp_r.at[i - 1],
                      first_dev(4 - offsets[i]))

    def combine(i):
        for q in range(1, 8):
            result_copy(i, q).wait_recv()

        @pl.loop(0, width // tile)
        def _(n):
            cols = pl.ds(pl.multiple_of(n * tile, tile), tile)
            part = lax.dot_general(ct_s[i], returned[i, :, cols], (((0,), (0,)), ((), ())),
                                   preferred_element_type=jnp.float32)
            if i == 0:
                acc[:, cols] = acc[:, cols] + part
            else:
                psend[i - 1, :, cols] = part.astype(jnp.bfloat16)
        if i:
            partial_copy(i).start()

    def forward(i):
        h = 0 if i == 1 else 1
        rows = pl.ds(h * half, half)
        return remote(xbuf.at[i, rows], xbuf.at[3, rows], sa_x.at[3, h], ra_x.at[3, h],
                      first_dev(1 if i == 1 else 3))

    make_tables(0)
    dispatch(0)
    x_copies[0].wait_recv()
    forward(1).start()
    x_copies[1].wait_recv()
    forward(2).start()
    for i in (1, 2, 3):
        r_copies[i - 1].wait_recv()
        if i == 3:
            forward(1).wait_recv()
            forward(2).wait_recv()
        else:
            x_copies[2 + i - 1].wait_recv()
        make_tables(i)
        dispatch(i)
        expert(i - 1)
        if i >= 2:
            combine(i - 2)
    expert(3)
    combine(2)
    combine(3)
    for i in (1, 2, 3):
        partial_copy(i).wait_recv()
    out_ref[...] = (acc[...] + precv[0].astype(jnp.float32) + precv[1].astype(jnp.float32)
                    + precv[2].astype(jnp.float32)).astype(jnp.bfloat16)
    for cp in x_copies + r_copies:
        cp.wait_send()
    forward(1).wait_send()
    forward(2).wait_send()
    for i in range(4):
        for q in range(1, 8):
            pack_copy(i, q).wait_send()
            result_copy(i, q).wait_send()
        if i:
            partial_copy(i).wait_send()


def moe(hidden, expert_norm_gain, routes, router, expert_gate_up, expert_down):
    tokens, width = hidden.shape
    experts = router.shape[1]
    routes_t = jnp.concatenate(
        [routes.T, jnp.full((8 - TOPK, tokens), -1, jnp.int32)], axis=0)
    bf, f32 = jnp.bfloat16, jnp.float32
    rows = 8 * CAP
    dma = pltpu.SemaphoreType.DMA
    return pl.pallas_call(
        moe_kernel,
        out_shape=jax.ShapeDtypeStruct((tokens, width), bf),
        in_specs=[pl.BlockSpec(memory_space=pltpu.VMEM)] * 6,
        out_specs=pl.BlockSpec(memory_space=pltpu.VMEM),
        scratch_shapes=[
            pltpu.VMEM((4, tokens, width), bf),
            pltpu.VMEM((4, 8, tokens), jnp.int32),
            pltpu.VMEM((4, experts, tokens), f32),
            pltpu.VMEM((4, experts, tokens), f32),
            pltpu.VMEM((4, rows, tokens), bf),
            pltpu.VMEM((4, rows, width), bf),
            pltpu.VMEM((4, rows, width), bf),
            pltpu.VMEM((rows, FFE), bf),
            pltpu.VMEM((4, rows, width), bf),
            pltpu.VMEM((4, rows, width), bf),
            pltpu.VMEM((3, tokens, width), bf),
            pltpu.VMEM((3, tokens, width), bf),
            pltpu.VMEM((tokens, width), f32),
            dma((4, 2)), dma((4, 2)), dma((4,)), dma((4,)),
            dma((4, 8)), dma((4, 8)), dma((4, 8)), dma((4, 8)),
            dma((3,)), dma((3,)),
        ],
        compiler_params=pltpu.CompilerParams(
            collective_id=1, has_side_effects=True, vmem_limit_bytes=60 * 1024 * 1024),
        name="moe",
    )(hidden, expert_norm_gain.reshape(1, width), routes_t, router.T,
      expert_gate_up.reshape(expert_gate_up.shape[-2:]), expert_down.reshape(expert_down.shape[-2:]))


def on_device(
    tokens,
    token_request_slot,
    request_prompt,
    request_adapter,
    prompt_page_table,
    shared_prompt_cache,
    routes,
    attention_norm_gain,
    query_matrix,
    key_value_weight,
    attention_output_weight,
    adapter_query_down,
    adapter_query_up,
    adapter_output_down,
    adapter_output_up,
    expert_norm_gain,
    router,
    expert_gate_up,
    expert_down,
):
    hidden_state = front(
        token_request_slot, request_prompt, request_adapter, prompt_page_table, tokens,
        shared_prompt_cache, attention_norm_gain, query_matrix, key_value_weight,
        attention_output_weight, adapter_query_down, adapter_query_up, adapter_output_down,
        adapter_output_up,
    )
    return moe(hidden_state, expert_norm_gain, routes, router, expert_gate_up, expert_down)


def solution(mesh):
    return jax.shard_map(
        on_device,
        mesh=mesh,
        in_specs=(
            P(("req", "exp"), None),
            P(("req", "exp"), None),
            P(("req", "exp")),
            P(("req", "exp")),
            P(),
            P(("req", "exp"), None, None),
            P(("req", "exp"), None),
            P(),
            P(),
            P(),
            P(),
            P(),
            P(),
            P(),
            P(),
            P(),
            P(),
            P("exp", None, None),
            P("exp", None, None),
        ),
        out_specs=P(("req", "exp"), None),
        check_vma=False,
    )
```

```python
import math

import jax
import jax.numpy as jnp
from jax import lax
from jax.experimental import pallas as pl
from jax.experimental.pallas import tpu as pltpu
from jax.sharding import PartitionSpec as P

MESH = pl.DeviceIdType.MESH
CAP = 48
FFE = 768

QUERY_HEADS = 12
KEY_VALUE_HEADS = 2
HEAD_WIDTH = 128
TOPK = 4
ADAPTER_RANK = 16
PPP = 16
PROMPT_LENGTH = 256


EPSILON = 1e-06
THETA = 1000000.0
VERY_NEGATIVE = -1e30


TILE_GROUPS = ((0, 6), (6, 5), (11, 5))
AXIS_ORDERS = ((0, 1, 2), (1, 2, 0), (2, 0, 1))


def layer_kernel(
    slot_ref, prompt_ref, adapter_ref, table_ref, tokens_ref, cache_ref, gain_ref,
    routes_ref, expert_gain_ref, router_ref,
    wq_any, wkv_any, aqd_any, aqu_any, wo_any, aod_any, aou_any, wgu_any, wdn_any,
    out_ref,
    cache, wq, wkv, aqd, aqu, wo, aod, aou, wgu_ref, wdn_ref,
    normed, inner_s, cos_s, sin_s, q_s, k_s, v_s, kv_s, att,
    xbuf, rbuf, rank_s, gate_s, ct_s, arrived, units, returned, psend, precv, acc,
    w_sem, c_sem, ag_s, ag_r, co_s, co_r,
    sa_x, ra_x, sa_r, ra_r, sb_p, rb_p, sb_r, rb_r, sp_s, sp_r,
):
    pack, result = wo, wq
    x = lax.axis_index("req")
    e_me = lax.axis_index("exp")
    y = e_me // 8
    z = lax.rem(e_me // 2, 4)
    c = lax.rem(e_me, 2)
    here = (x, y, z)

    def device(axis, offset):
        p = list(here)
        p[axis] = lax.rem(p[axis] + offset, 4)
        return (p[0], (p[1] * 4 + p[2]) * 2 + c)

    partner = (x, (y * 4 + z) * 2 + 1 - c)

    barrier = pltpu.get_barrier_semaphore()
    for off in (1, 2, 3):
        pl.semaphore_signal(barrier, 1, device_id=device(0, off), device_id_type=MESH)
    for dy in range(4):
        for dc in range(2):
            if dy or dc:
                dev = (x, (lax.rem(y + dy, 4) * 4 + z) * 2 + lax.rem(c + dc, 2))
                pl.semaphore_signal(barrier, 1, device_id=dev, device_id_type=MESH)
    for dz in range(1, 4):
        for dc in range(2):
            dev = (x, (y * 4 + lax.rem(z + dz, 4)) * 2 + lax.rem(c + dc, 2))
            pl.semaphore_signal(barrier, 1, device_id=dev, device_id_type=MESH)

    first_pos = y * (1 - c) + z * c
    first_base = z * 2 * (1 - c) + y * 8 * c + c
    first_step = 8 - 6 * c
    second_pos = z * (1 - c) + y * c
    second_base = y * 8 * (1 - c) + z * 2 * c
    second_step = 2 + 6 * c

    def first_dev(offset):
        return (x, first_base + lax.rem(first_pos + offset, 4) * first_step)

    def second_exp(offset, dc):
        return second_base + lax.rem(second_pos + offset, 4) * second_step + lax.rem(c + dc, 2)

    def relay_dev(j, dc):
        rc = lax.rem(c + dc, 2)
        pos = z * (1 - rc) + y * rc
        base = y * 8 * (1 - rc) + z * 2 * rc
        return (x, base + lax.rem(pos - j + 4, 4) * (2 + 6 * rc) + rc)

    def remote(src, dst, ssem, rsem, dev):
        return pltpu.make_async_remote_copy(
            src_ref=src, dst_ref=dst, send_sem=ssem, recv_sem=rsem,
            device_id=dev, device_id_type=MESH)

    own = []
    for p in range(4):
        for col in range(4):
            cp = pltpu.make_async_copy(
                cache_ref.at[p, :, pl.ds(col * 128, 128)],
                cache.at[x, y, z, c, p * 4 + col], c_sem.at[p * 4 + col])
            cp.start()
            own.append(cp)
    weights = []
    for i, (src, dst) in enumerate((
            (wkv_any, wkv), (aqd_any, aqd), (aqu_any, aqu), (wq_any, wq),
            (aod_any, aod), (wo_any, wo), (aou_any, aou), (wgu_any, wgu_ref), (wdn_any, wdn_ref))):
        cp = pltpu.make_async_copy(src, dst, w_sem.at[i])
        cp.start()
        weights.append(cp)

    def block(where, first, count):
        return cache.at[where[0], where[1], where[2], c, pl.ds(first, count)]

    def step(g, phase, kind, axis, where):
        lo, n = TILE_GROUPS[g]
        if kind == 2:
            n = n // 2
        elif kind == 3:
            lo, n = lo + n // 2, n - n // 2
        view = block(where, lo, n)
        return pltpu.make_async_remote_copy(
            src_ref=view, dst_ref=view, send_sem=ag_s.at[g, phase, kind], recv_sem=ag_r.at[g, phase, kind],
            device_id=device(axis, {0: 1, 2: 1, 4: 2}.get(kind, 3)), device_id_type=MESH)

    every = slice(None)

    def place(g, second, third):
        order = AXIS_ORDERS[g]
        w = [every, every, every]
        for axis, off in ((order[1], second), (order[2], third)):
            if off is not None:
                w[axis] = lax.rem(here[axis] + off, 4)
        return w

    class Ring:
        def __init__(self, g, phase, axis, where_of):
            self.g, self.phase, self.axis, self.where_of = g, phase, axis, where_of

        def cp(self, kind, off):
            return step(self.g, self.phase, kind, self.axis, self.where_of(off))

        def begin(self):
            self.cp(0, 0).start()
            self.cp(1, 0).start()

        def pass_on(self):
            self.cp(0, 3).wait_recv()
            self.cp(2, 3).start()
            self.cp(1, 1).wait_recv()
            self.cp(3, 1).start()

        def finish(self):
            self.cp(2, 2).wait_recv()
            self.cp(3, 2).wait_recv()

        def drain(self):
            self.cp(0, 0).wait_send()
            self.cp(1, 0).wait_send()
            self.cp(2, 3).wait_send()
            self.cp(3, 1).wait_send()

    class Short(Ring):
        def begin(self):
            for kind in (0, 1, 4):
                self.cp(kind, 0).start()

        def near(self):
            self.cp(0, 3).wait_recv()
            self.cp(1, 1).wait_recv()

        def finish(self):
            self.cp(4, 2).wait_recv()

        def drain(self):
            for kind in (0, 1, 4):
                self.cp(kind, 0).wait_send()

    def first_where(g):
        def f(off):
            order = AXIS_ORDERS[g]
            w = [here[0], here[1], here[2]]
            w[order[0]] = lax.rem(here[order[0]] + off, 4)
            return w
        return f

    groups = range(3)
    ring1 = [Short(g, 0, AXIS_ORDERS[g][0], first_where(g)) for g in groups]
    ring2 = [Short(g, 1, AXIS_ORDERS[g][1], lambda off, g=g: place(g, off, 0)) for g in groups]
    ring3 = [[Ring(g, 2 + o, AXIS_ORDERS[g][2], lambda off, g=g, o=o: place(g, o, off)) for o in range(4)]
             for g in groups]

    def share(g, i, second, third):
        lo, n = TILE_GROUPS[g]
        view = block(place(g, second, third), lo, n)
        return pltpu.make_async_remote_copy(
            src_ref=view, dst_ref=view, send_sem=co_s.at[g, i], recv_sem=co_r.at[g, i],
            device_id=partner, device_id_type=MESH)

    def share_mine(g, i):
        if i == 0:
            return share(g, 0, None, 0)
        return share(g, i, (i - 1) // 3, 1 + (i - 1) % 3)

    def theirs(g, i):
        lo, n = TILE_GROUPS[g]
        second, third = (None, 0) if i == 0 else ((i - 1) // 3, 1 + (i - 1) % 3)
        w = place(g, second, third)
        view = cache.at[w[0], w[1], w[2], 1 - c, pl.ds(lo, n)]
        return pltpu.make_async_remote_copy(
            src_ref=view, dst_ref=view, send_sem=co_s.at[g, i], recv_sem=co_r.at[g, i],
            device_id=partner, device_id_type=MESH)

    tokens = tokens_ref.shape[0]
    width = tokens_ref.shape[1]
    half_rows = tokens // 2

    tv = tokens_ref[...].astype(jnp.float32)
    factor = lax.rsqrt(jnp.mean(tv * tv, axis=-1, keepdims=True) + EPSILON)
    gain = gain_ref[...].astype(jnp.float32).reshape(1, width)
    normed[...] = (tv * factor * gain).astype(jnp.bfloat16)

    for cp in own:
        cp.wait()
    pl.semaphore_wait(barrier, 16)
    for g in groups:
        ring1[g].begin()

    slot_row = slot_ref[...]
    index_col = lax.broadcasted_iota(jnp.int32, (tokens, 1), 0).astype(jnp.float32)
    slot_col = jnp.zeros((tokens, 1), jnp.float32)
    start_col = jnp.zeros((tokens, 1), jnp.float32)
    adapter_col = jnp.zeros((tokens, 1), jnp.int32) + adapter_ref[0]
    for r in range(1, 4):
        start = jnp.sum(jnp.where(slot_row < r, 1.0, 0.0), axis=1, keepdims=True)
        reached = index_col >= start
        slot_col = jnp.where(reached, float(r), slot_col)
        start_col = jnp.where(reached, start, start_col)
        adapter_col = jnp.where(reached, adapter_ref[r], adapter_col)
    position = index_col - start_col + float(PROMPT_LENGTH)
    lane = lax.broadcasted_iota(jnp.int32, (1, HEAD_WIDTH), 1)
    pair = lax.rem(lane, HEAD_WIDTH // 2).astype(jnp.float32)
    frequency = jnp.exp(pair * (-math.log(THETA) / (HEAD_WIDTH // 2)))
    angle = position * frequency
    cos_s[...] = jnp.cos(angle)
    sin_s[...] = jnp.where(lane < HEAD_WIDTH // 2, -jnp.sin(angle), jnp.sin(angle))

    def rotate(v):
        return v * cos_s[...] + pltpu.roll(v, HEAD_WIDTH // 2, 1) * sin_s[...]

    for g in groups:
        ring1[g].near()
        ring1[g].finish()
        ring2[g].begin()
    for g in groups:
        ring3[g][0].begin()

    weights[0].wait()
    kv = jnp.dot(normed[...], wkv[...], preferred_element_type=jnp.float32)
    for h in range(2):
        k_s[h] = rotate(kv[:, h * 128:(h + 1) * 128]).astype(jnp.bfloat16)
        v_s[h] = kv[:, 256 + h * 128:256 + (h + 1) * 128].astype(jnp.bfloat16)

    for g in groups:
        ring2[g].near()
        ring3[g][3].begin()
        ring3[g][1].begin()
    for g in groups:
        ring2[g].finish()
        ring3[g][2].begin()
        share_mine(g, 0).start()

    owner = lax.broadcasted_iota(jnp.int32, (tokens, aqd.shape[1]), 1) // ADAPTER_RANK
    mine = owner == adapter_col
    weights[1].wait()
    inner = jnp.dot(normed[...], aqd[...], preferred_element_type=jnp.float32)
    inner_s[...] = jnp.where(mine, inner, 0.0).astype(jnp.bfloat16)
    weights[2].wait()
    weights[3].wait()

    def queries(lo, hi):
        @pl.loop(lo, hi)
        def _(n):
            cols = pl.ds(pl.multiple_of(n * 256, 256), 256)
            qv = jnp.dot(normed[...], wq[:, cols], preferred_element_type=jnp.float32)
            qv = qv + jnp.dot(inner_s[...], aqu[:, cols], preferred_element_type=jnp.float32)
            for h in range(2):
                q_s[n * 2 + h] = rotate(qv[:, h * 128:(h + 1) * 128]).astype(jnp.bfloat16)

    queries(0, 3)
    for g in groups:
        ring3[g][0].pass_on()
        for third in (0, 2):
            share_mine(g, 1 + third).start()
    queries(3, 6)

    row_i = lax.broadcasted_iota(jnp.int32, (tokens, tokens), 0)
    col_i = lax.broadcasted_iota(jnp.int32, (tokens, tokens), 1)
    eye = jnp.where(row_i == col_i, 1.0, 0.0).astype(jnp.bfloat16)
    rbuf[0] = jnp.full(rbuf.shape[1:], -1.0, jnp.float32)
    rbuf[0, 0:TOPK, :] = lax.dot_general(
        routes_ref[...].astype(jnp.float32).astype(jnp.bfloat16), eye, (((0,), (0,)), ((), ())),
        preferred_element_type=jnp.float32)

    for o, before in ((3, 0), (1, 3), (2, 1)):
        for g in groups:
            ring3[g][o].pass_on()
            for third in (0, 2):
                share_mine(g, 1 + o * 3 + third).start()
            ring3[g][before].finish()
            share_mine(g, 1 + before * 3 + 1).start()
    r_copies = []
    for i, off in ((1, 1), (2, 3), (3, 2)):
        cp = remote(rbuf.at[0], rbuf.at[i], sa_r.at[i], ra_r.at[i], first_dev(off))
        cp.start()
        r_copies.append(cp)
    for g in groups:
        ring3[g][2].finish()
        share_mine(g, 1 + 2 * 3 + 1).start()
    for g in groups:
        for i in range(13):
            theirs(g, i).wait_recv()

    @pl.loop(0, 4)
    def _(r):
        base = prompt_ref[r] * PPP
        for j in range(PPP):
            page = table_ref[base + j]
            d = page // 4
            px, py, pz, pc = d // 32, lax.rem(d // 8, 4), lax.rem(d // 2, 4), lax.rem(d, 2)
            t = lax.rem(page, 4) * 4
            for col in range(4):
                kv_s[col, r, pl.ds(j * 16, 16), :] = cache[px, py, pz, pc, t + col]

    scale = HEAD_WIDTH ** (-0.5)
    group = QUERY_HEADS // KEY_VALUE_HEADS
    nt = (((1,), (1,)), ((), ()))

    before_m = jnp.where(row_i < col_i, 1.0, 0.0).astype(jnp.bfloat16)
    half = half_rows
    offsets = (0, 1, 3, 2)

    def x_copy(i, h):
        rows = pl.ds(h * half, half)
        return remote(xbuf.at[0, rows], xbuf.at[i, rows], sa_x.at[i, h], ra_x.at[i, h],
                      first_dev(offsets[i]))

    def attend(b):
        @pl.loop(0, KEY_VALUE_HEADS)
        def _(h):
            rows = slice(b * half_rows, (b + 1) * half_rows)
            keys = (b + 1) * half_rows
            q = q_s[pl.ds(h * group, group), rows, :].reshape(group * half_rows, HEAD_WIDTH)
            slot = slot_col[rows]
            ki = lax.broadcasted_iota(jnp.int32, (half_rows, keys), 1).astype(jnp.float32)
            ok = jnp.logical_and(ki <= index_col[rows], ki >= start_col[rows])
            local = lax.dot_general(q, k_s[h, 0:keys], nt, preferred_element_type=jnp.float32)
            local = local.reshape(group, half_rows, keys) * scale
            local = jnp.where(ok[None], local, VERY_NEGATIVE)
            picked = None
            for r in range(b, b + 3):
                s = lax.dot_general(q, kv_s[h, r], nt, preferred_element_type=jnp.float32)
                s = s.reshape(group, half_rows, PROMPT_LENGTH)
                picked = s if picked is None else jnp.where((slot == float(r))[None], s, picked)
            picked = picked * scale
            top = jnp.maximum(jnp.max(picked, axis=-1, keepdims=True), jnp.max(local, axis=-1, keepdims=True))
            wp = jnp.exp(picked - top)
            wl = jnp.exp(local - top)
            total = jnp.sum(wp, axis=-1, keepdims=True) + jnp.sum(wl, axis=-1, keepdims=True)
            wp = wp.astype(jnp.bfloat16).reshape(group * half_rows, PROMPT_LENGTH)
            wl = wl.astype(jnp.bfloat16).reshape(group * half_rows, keys)
            summed = None
            for r in range(b, b + 3):
                o = jnp.dot(wp, kv_s[KEY_VALUE_HEADS + h, r], preferred_element_type=jnp.float32)
                o = o.reshape(group, half_rows, HEAD_WIDTH)
                summed = o if summed is None else jnp.where((slot == float(r))[None], o, summed)
            o = jnp.dot(wl, v_s[h, 0:keys], preferred_element_type=jnp.float32)
            summed = (summed + o.reshape(group, half_rows, HEAD_WIDTH)) / total
            for i in range(group):
                col = pl.multiple_of((h * group + i) * HEAD_WIDTH, HEAD_WIDTH)
                att[rows, pl.ds(col, HEAD_WIDTH)] = summed[i].astype(jnp.bfloat16)

    def project(b):
        rows = slice(b * half_rows, (b + 1) * half_rows)
        inner = jnp.dot(att[rows], aod[...], preferred_element_type=jnp.float32)
        inner_s[rows] = jnp.where(mine[rows], inner, 0.0).astype(jnp.bfloat16)

        @pl.loop(0, width // 512)
        def _(n):
            cols = pl.ds(pl.multiple_of(n * 512, 512), 512)
            mix = jnp.dot(att[rows], wo[:, cols], preferred_element_type=jnp.float32)
            mix = mix + jnp.dot(inner_s[rows], aou[:, cols], preferred_element_type=jnp.float32)
            hid = (tokens_ref[rows, cols].astype(jnp.float32) + mix).astype(jnp.bfloat16)
            acc[rows, cols] = hid.astype(jnp.float32)

        hv = acc[rows]
        factor = lax.rsqrt(jnp.mean(hv * hv, axis=-1, keepdims=True) + EPSILON)
        xbuf[0, rows] = (hv * factor * expert_gain).astype(jnp.bfloat16)

    expert_gain = expert_gain_ref[...].astype(jnp.float32).reshape(1, width)
    attend(0)
    for cp in weights[4:7]:
        cp.wait()
    for b in range(2):
        if b:
            attend(b)
        project(b)
        x_copy(1, b).start()
        x_copy(2, b).start()

    experts = router_ref.shape[0]

    def make_tables(i):
        r = rbuf[i]
        ei = lax.broadcasted_iota(jnp.int32, (experts, tokens), 0).astype(jnp.float32)
        hit = ei == r[0:1, :]
        for k in range(1, TOPK):
            hit = jnp.logical_or(hit, ei == r[k:k + 1, :])
        hit_f = jnp.where(hit, 1.0, 0.0)
        rank = jnp.dot(hit_f.astype(jnp.bfloat16), before_m, preferred_element_type=jnp.float32)
        rank_s[i] = jnp.where(hit, rank, -1.0)
        logits = lax.dot_general(router_ref[...], xbuf[i], (((1,), (1,)), ((), ())),
                                 preferred_element_type=jnp.float32)
        sig = jnp.where(hit, jax.nn.sigmoid(logits), 0.0)
        gate_s[i] = sig / jnp.sum(sig, axis=0, keepdims=True)

    slot_i = lax.broadcasted_iota(jnp.int32, (CAP, tokens), 0).astype(jnp.float32)
    tile = 512

    def dispatch(i):
        picks = []
        for j in range(4):
            for dc in range(2):
                e = second_exp(j, dc)
                rank_row = rank_s[i, pl.ds(e, 1), :]
                gate_row = gate_s[i, pl.ds(e, 1), :]
                eq = slot_i == rank_row
                picks.append(jnp.where(eq, 1.0, 0.0).astype(jnp.bfloat16))
                q = j * 2 + dc
                ct_s[i, q * CAP:(q + 1) * CAP, :] = jnp.where(eq, gate_row, 0.0).astype(jnp.bfloat16)
        pick = jnp.concatenate(picks, axis=0)

        @pl.loop(0, width // tile)
        def _(n):
            cols = pl.ds(pl.multiple_of(n * tile, tile), tile)
            rows = jnp.dot(pick, xbuf[i, :, cols], preferred_element_type=jnp.float32).astype(jnp.bfloat16)
            arrived[i, 0:CAP, cols] = rows[0:CAP]
            pack[i * 8 * CAP:(i + 1) * 8 * CAP, cols] = rows
        for q in range(1, 8):
            pack_copy(i, q).start()

    def pack_copy(i, q):
        j, dc = q // 2, q % 2
        return remote(pack.at[pl.ds((i * 8 + q) * CAP, CAP)], arrived.at[i, pl.ds(q * CAP, CAP)],
                      sb_p.at[i, q], rb_p.at[i, q], (x, second_exp(j, dc)))

    def result_copy(i, q):
        j, dc = q // 2, q % 2
        return remote(result.at[pl.ds((i * 8 + q) * CAP, CAP)], returned.at[i, pl.ds(q * CAP, CAP)],
                      sb_r.at[i, q], rb_r.at[i, q], relay_dev(j, dc))

    def expert(i):
        for q in range(1, 8):
            pack_copy(i, q).wait_recv()

        @pl.loop(0, FFE // 256)
        def _(n):
            up_cols = pl.ds(pl.multiple_of(FFE + n * 256, 256), 256)
            cols = pl.ds(pl.multiple_of(n * 256, 256), 256)
            a = arrived[i]
            g = jnp.dot(a, wgu_ref[:, cols], preferred_element_type=jnp.float32)
            u = jnp.dot(a, wgu_ref[:, up_cols], preferred_element_type=jnp.float32)
            units[:, cols] = (jnp.maximum(g, 0.0) * u).astype(jnp.bfloat16)

        @pl.loop(0, width // tile)
        def _(n):
            cols = pl.ds(pl.multiple_of(n * tile, tile), tile)
            rows = jnp.dot(units[...], wdn_ref[:, cols], preferred_element_type=jnp.float32).astype(jnp.bfloat16)
            returned[i, 0:CAP, cols] = rows[0:CAP]
            result[i * 8 * CAP:(i + 1) * 8 * CAP, cols] = rows
        for q in range(1, 8):
            result_copy(i, q).start()

    def partial_copy(i):
        return remote(psend.at[i - 1], precv.at[i - 1], sp_s.at[i - 1], sp_r.at[i - 1],
                      first_dev(4 - offsets[i]))

    def combine(i):
        for q in range(1, 8):
            result_copy(i, q).wait_recv()

        @pl.loop(0, width // tile)
        def _(n):
            cols = pl.ds(pl.multiple_of(n * tile, tile), tile)
            part = lax.dot_general(ct_s[i], returned[i, :, cols], (((0,), (0,)), ((), ())),
                                   preferred_element_type=jnp.float32)
            if i == 0:
                acc[:, cols] = acc[:, cols] + part
            else:
                psend[i - 1, :, cols] = part.astype(jnp.bfloat16)
        if i:
            partial_copy(i).start()

    def forward(i):
        h = 0 if i == 1 else 1
        rows = pl.ds(h * half, half)
        return remote(xbuf.at[i, rows], xbuf.at[3, rows], sa_x.at[3, h], ra_x.at[3, h],
                      first_dev(1 if i == 1 else 3))

    make_tables(0)
    dispatch(0)
    for cp in weights[7:]:
        cp.wait()
    x_copy(1, 0).wait_recv()
    forward(1).start()
    x_copy(2, 1).wait_recv()
    forward(2).start()
    for i in (1, 2, 3):
        r_copies[i - 1].wait_recv()
        if i == 3:
            forward(1).wait_recv()
            forward(2).wait_recv()
        else:
            x_copy(i, 1 if i == 1 else 0).wait_recv()
        make_tables(i)
        dispatch(i)
        expert(i - 1)
        if i >= 2:
            combine(i - 2)
    expert(3)
    combine(2)
    combine(3)
    for i in (1, 2, 3):
        partial_copy(i).wait_recv()
    out_ref[...] = (acc[...] + precv[0].astype(jnp.float32) + precv[1].astype(jnp.float32)
                    + precv[2].astype(jnp.float32)).astype(jnp.bfloat16)
    for cp in r_copies:
        cp.wait_send()
    for i in (1, 2):
        for h in range(2):
            x_copy(i, h).wait_send()
    forward(1).wait_send()
    forward(2).wait_send()
    for i in range(4):
        for q in range(1, 8):
            pack_copy(i, q).wait_send()
            result_copy(i, q).wait_send()
        if i:
            partial_copy(i).wait_send()
    for g in groups:
        ring1[g].drain()
        ring2[g].drain()
        for o in range(4):
            ring3[g][o].drain()
        for i in range(13):
            share_mine(g, i).wait_send()


def layer(slots, prompts, adapters, table, tokens, shard, gain, routes, expert_gain, router,
          wq, wkv, wo, aqd, aqu, aod, aou, wgu, wdn):
    rows, width = tokens.shape
    bf, f32 = jnp.bfloat16, jnp.float32
    dma = pltpu.SemaphoreType.DMA
    vmem = pl.BlockSpec(memory_space=pltpu.VMEM)
    smem = pl.BlockSpec(memory_space=pltpu.SMEM)
    hbm = pl.BlockSpec(memory_space=pl.ANY)
    experts = router.shape[1]
    ordered = (wq, wkv, aqd, aqu, wo, aod, aou, wgu.reshape(wgu.shape[-2:]), wdn.reshape(wdn.shape[-2:]))
    routed = 8 * CAP
    return pl.pallas_call(
        layer_kernel,
        out_shape=jax.ShapeDtypeStruct((rows, width), bf),
        in_specs=[vmem, smem, smem, smem, vmem, hbm, vmem, vmem, vmem, vmem] + [hbm] * 9,
        out_specs=vmem,
        scratch_shapes=[pltpu.VMEM((4, 4, 4, 2, 16, 16, 128), bf)]
        + [pltpu.VMEM(w.shape, bf) for w in ordered]
        + [
            pltpu.VMEM((rows, width), bf),
            pltpu.VMEM((rows, aqd.shape[1]), bf),
            pltpu.VMEM((rows, HEAD_WIDTH), f32),
            pltpu.VMEM((rows, HEAD_WIDTH), f32),
            pltpu.VMEM((QUERY_HEADS, rows, HEAD_WIDTH), bf),
            pltpu.VMEM((KEY_VALUE_HEADS, rows, HEAD_WIDTH), bf),
            pltpu.VMEM((KEY_VALUE_HEADS, rows, HEAD_WIDTH), bf),
            pltpu.VMEM((2 * KEY_VALUE_HEADS, 4, PROMPT_LENGTH, HEAD_WIDTH), bf),
            pltpu.VMEM((rows, width), bf),
            pltpu.VMEM((4, rows, width), bf),
            pltpu.VMEM((4, 8, rows), f32),
            pltpu.VMEM((4, experts, rows), f32),
            pltpu.VMEM((4, experts, rows), f32),
            pltpu.VMEM((4, routed, rows), bf),
            pltpu.VMEM((4, routed, width), bf),
            pltpu.VMEM((routed, FFE), bf),
            pltpu.VMEM((4, routed, width), bf),
            pltpu.VMEM((3, rows, width), bf),
            pltpu.VMEM((3, rows, width), bf),
            pltpu.VMEM((rows, width), f32),
            dma((9,)), dma((16,)), dma((3, 6, 5)), dma((3, 6, 5)), dma((3, 13)), dma((3, 13)),
            dma((4, 2)), dma((4, 2)), dma((4,)), dma((4,)),
            dma((4, 8)), dma((4, 8)), dma((4, 8)), dma((4, 8)),
            dma((3,)), dma((3,)),
        ],
        compiler_params=pltpu.CompilerParams(
            collective_id=1, has_side_effects=True, vmem_limit_bytes=63 * 1024 * 1024),
        name="layer",
    )(slots, prompts, adapters, table, tokens, shard, gain, routes, expert_gain, router.T, *ordered)


def on_device(
    tokens,
    token_request_slot,
    request_prompt,
    request_adapter,
    prompt_page_table,
    shared_prompt_cache,
    routes,
    attention_norm_gain,
    query_matrix,
    key_value_weight,
    attention_output_weight,
    adapter_query_down,
    adapter_query_up,
    adapter_output_down,
    adapter_output_up,
    expert_norm_gain,
    router,
    expert_gate_up,
    expert_down,
):
    return layer(
        token_request_slot, request_prompt, request_adapter, prompt_page_table, tokens,
        shared_prompt_cache, attention_norm_gain, routes, expert_norm_gain, router,
        query_matrix, key_value_weight, attention_output_weight, adapter_query_down,
        adapter_query_up, adapter_output_down, adapter_output_up, expert_gate_up, expert_down,
    )


def solution(mesh):
    return jax.shard_map(
        on_device,
        mesh=mesh,
        in_specs=(
            P(("req", "exp"), None),
            P(("req", "exp"), None),
            P(("req", "exp")),
            P(("req", "exp")),
            P(),
            P(("req", "exp"), None, None),
            P(("req", "exp"), None),
            P(),
            P(),
            P(),
            P(),
            P(),
            P(),
            P(),
            P(),
            P(),
            P(),
            P("exp", None, None),
            P("exp", None, None),
        ),
        out_specs=P(("req", "exp"), None),
        check_vma=False,
    )
```

```python
import math

import jax
import jax.numpy as jnp
from jax import lax
from jax.experimental import pallas as pl
from jax.experimental.pallas import tpu as pltpu
from jax.sharding import PartitionSpec as P

MESH = pl.DeviceIdType.MESH
CAP = 48
FFE = 768

QUERY_HEADS = 12
KEY_VALUE_HEADS = 2
HEAD_WIDTH = 128
TOPK = 4
ADAPTER_RANK = 16
PPP = 16
PROMPT_LENGTH = 256


EPSILON = 1e-06
THETA = 1000000.0
VERY_NEGATIVE = -1e30


TILE_GROUPS = ((0, 6), (6, 5), (11, 5))
AXIS_ORDERS = ((0, 1, 2), (1, 2, 0), (2, 0, 1))


def layer_kernel(
    slot_ref, prompt_ref, adapter_ref, table_ref, tokens_any, cache_ref, gain_ref,
    routes_ref, expert_gain_ref, router_ref,
    wq_any, wkv_any, aqd_any, aqu_any, wo_any, aod_any, aou_any, wgu_any, wdn_any,
    out_ref,
    cache, tokens_ref, wq, wkv, aqd, aqu, wo, aod, aou, wgu_ref, wdn_ref,
    normed, inner_s, cos_s, sin_s, q_s, k_s, v_s, kv_s, att,
    xbuf, rbuf, rank_s, gate_s, ct_s, arrived, units, returned, psend, precv, acc,
    w_sem, c_sem, ag_s, ag_r, co_s, co_r,
    sa_x, ra_x, sa_r, ra_r, sb_p, rb_p, sb_r, rb_r, sp_s, sp_r,
):
    pack, result = wo, wq
    x = lax.axis_index("req")
    e_me = lax.axis_index("exp")
    y = e_me // 8
    z = lax.rem(e_me // 2, 4)
    c = lax.rem(e_me, 2)
    here = (x, y, z)

    def device(axis, offset):
        p = list(here)
        p[axis] = lax.rem(p[axis] + offset, 4)
        return (p[0], (p[1] * 4 + p[2]) * 2 + c)

    partner = (x, (y * 4 + z) * 2 + 1 - c)

    barrier = pltpu.get_barrier_semaphore()
    for off in (1, 2, 3):
        pl.semaphore_signal(barrier, 1, device_id=device(0, off), device_id_type=MESH)
    for dy in range(4):
        for dc in range(2):
            if dy or dc:
                dev = (x, (lax.rem(y + dy, 4) * 4 + z) * 2 + lax.rem(c + dc, 2))
                pl.semaphore_signal(barrier, 1, device_id=dev, device_id_type=MESH)
    for dz in range(1, 4):
        for dc in range(2):
            dev = (x, (y * 4 + lax.rem(z + dz, 4)) * 2 + lax.rem(c + dc, 2))
            pl.semaphore_signal(barrier, 1, device_id=dev, device_id_type=MESH)

    first_pos = y * (1 - c) + z * c
    first_base = z * 2 * (1 - c) + y * 8 * c + c
    first_step = 8 - 6 * c
    second_pos = z * (1 - c) + y * c
    second_base = y * 8 * (1 - c) + z * 2 * c
    second_step = 2 + 6 * c

    def first_dev(offset):
        return (x, first_base + lax.rem(first_pos + offset, 4) * first_step)

    def second_exp(offset, dc):
        return second_base + lax.rem(second_pos + offset, 4) * second_step + lax.rem(c + dc, 2)

    def relay_dev(j, dc):
        rc = lax.rem(c + dc, 2)
        pos = z * (1 - rc) + y * rc
        base = y * 8 * (1 - rc) + z * 2 * rc
        return (x, base + lax.rem(pos - j + 4, 4) * (2 + 6 * rc) + rc)

    def remote(src, dst, ssem, rsem, dev):
        return pltpu.make_async_remote_copy(
            src_ref=src, dst_ref=dst, send_sem=ssem, recv_sem=rsem,
            device_id=dev, device_id_type=MESH)

    own = []
    for p in range(4):
        for col in range(4):
            cp = pltpu.make_async_copy(
                cache_ref.at[p, :, pl.ds(col * 128, 128)],
                cache.at[x, y, z, c, p * 4 + col], c_sem.at[p * 4 + col])
            cp.start()
            own.append(cp)
    token_copy = pltpu.make_async_copy(tokens_any, tokens_ref, w_sem.at[9])
    token_copy.start()
    weights = []
    for i, (src, dst) in enumerate((
            (wkv_any, wkv), (aqd_any, aqd), (aqu_any, aqu), (wq_any, wq),
            (aod_any, aod), (wo_any, wo), (aou_any, aou), (wgu_any, wgu_ref), (wdn_any, wdn_ref))):
        cp = pltpu.make_async_copy(src, dst, w_sem.at[i])
        cp.start()
        weights.append(cp)

    def block(where, first, count):
        return cache.at[where[0], where[1], where[2], c, pl.ds(first, count)]

    def step(g, phase, kind, axis, where):
        lo, n = TILE_GROUPS[g]
        if kind == 2:
            n = n // 2
        elif kind == 3:
            lo, n = lo + n // 2, n - n // 2
        view = block(where, lo, n)
        return pltpu.make_async_remote_copy(
            src_ref=view, dst_ref=view, send_sem=ag_s.at[g, phase, kind], recv_sem=ag_r.at[g, phase, kind],
            device_id=device(axis, {0: 1, 2: 1, 4: 2}.get(kind, 3)), device_id_type=MESH)

    every = slice(None)

    def place(g, second, third):
        order = AXIS_ORDERS[g]
        w = [every, every, every]
        for axis, off in ((order[1], second), (order[2], third)):
            if off is not None:
                w[axis] = lax.rem(here[axis] + off, 4)
        return w

    class Ring:
        def __init__(self, g, phase, axis, where_of):
            self.g, self.phase, self.axis, self.where_of = g, phase, axis, where_of

        def cp(self, kind, off):
            return step(self.g, self.phase, kind, self.axis, self.where_of(off))

        def begin(self):
            self.cp(0, 0).start()
            self.cp(1, 0).start()

        def pass_on(self):
            self.cp(0, 3).wait_recv()
            self.cp(2, 3).start()
            self.cp(1, 1).wait_recv()
            self.cp(3, 1).start()

        def finish(self):
            self.cp(2, 2).wait_recv()
            self.cp(3, 2).wait_recv()

        def drain(self):
            self.cp(0, 0).wait_send()
            self.cp(1, 0).wait_send()
            self.cp(2, 3).wait_send()
            self.cp(3, 1).wait_send()

    class Short(Ring):
        def begin(self):
            for kind in (0, 1, 4):
                self.cp(kind, 0).start()

        def near(self):
            self.cp(0, 3).wait_recv()
            self.cp(1, 1).wait_recv()

        def finish(self):
            self.cp(4, 2).wait_recv()

        def drain(self):
            for kind in (0, 1, 4):
                self.cp(kind, 0).wait_send()

    def first_where(g):
        def f(off):
            order = AXIS_ORDERS[g]
            w = [here[0], here[1], here[2]]
            w[order[0]] = lax.rem(here[order[0]] + off, 4)
            return w
        return f

    groups = range(3)
    ring1 = [Short(g, 0, AXIS_ORDERS[g][0], first_where(g)) for g in groups]
    ring2 = [Short(g, 1, AXIS_ORDERS[g][1], lambda off, g=g: place(g, off, 0)) for g in groups]
    ring3 = [[Ring(g, 2 + o, AXIS_ORDERS[g][2], lambda off, g=g, o=o: place(g, o, off)) for o in range(4)]
             for g in groups]

    def share(g, i, second, third):
        lo, n = TILE_GROUPS[g]
        view = block(place(g, second, third), lo, n)
        return pltpu.make_async_remote_copy(
            src_ref=view, dst_ref=view, send_sem=co_s.at[g, i], recv_sem=co_r.at[g, i],
            device_id=partner, device_id_type=MESH)

    def share_mine(g, i):
        if i == 0:
            return share(g, 0, None, 0)
        return share(g, i, (i - 1) // 3, 1 + (i - 1) % 3)

    def theirs(g, i):
        lo, n = TILE_GROUPS[g]
        second, third = (None, 0) if i == 0 else ((i - 1) // 3, 1 + (i - 1) % 3)
        w = place(g, second, third)
        view = cache.at[w[0], w[1], w[2], 1 - c, pl.ds(lo, n)]
        return pltpu.make_async_remote_copy(
            src_ref=view, dst_ref=view, send_sem=co_s.at[g, i], recv_sem=co_r.at[g, i],
            device_id=partner, device_id_type=MESH)

    tokens = tokens_ref.shape[0]
    width = tokens_ref.shape[1]
    half_rows = tokens // 2

    for cp in own:
        cp.wait()
    pl.semaphore_wait(barrier, 16)
    for g in groups:
        ring1[g].begin()

    token_copy.wait()
    tv = tokens_ref[...].astype(jnp.float32)
    factor = lax.rsqrt(jnp.mean(tv * tv, axis=-1, keepdims=True) + EPSILON)
    gain = gain_ref[...].astype(jnp.float32).reshape(1, width)
    normed[...] = (tv * factor * gain).astype(jnp.bfloat16)

    for g in groups:
        ring1[g].near()
        ring1[g].finish()
        ring2[g].begin()
    for g in groups:
        ring3[g][0].begin()

    slot_row = slot_ref[...]
    index_col = lax.broadcasted_iota(jnp.int32, (tokens, 1), 0).astype(jnp.float32)
    slot_col = jnp.zeros((tokens, 1), jnp.float32)
    start_col = jnp.zeros((tokens, 1), jnp.float32)
    adapter_col = jnp.zeros((tokens, 1), jnp.int32) + adapter_ref[0]
    for r in range(1, 4):
        start = jnp.sum(jnp.where(slot_row < r, 1.0, 0.0), axis=1, keepdims=True)
        reached = index_col >= start
        slot_col = jnp.where(reached, float(r), slot_col)
        start_col = jnp.where(reached, start, start_col)
        adapter_col = jnp.where(reached, adapter_ref[r], adapter_col)
    position = index_col - start_col + float(PROMPT_LENGTH)
    lane = lax.broadcasted_iota(jnp.int32, (1, HEAD_WIDTH), 1)
    pair = lax.rem(lane, HEAD_WIDTH // 2).astype(jnp.float32)
    frequency = jnp.exp(pair * (-math.log(THETA) / (HEAD_WIDTH // 2)))
    angle = position * frequency
    cos_s[...] = jnp.cos(angle)

    def rotate(v):
        return v * cos_s[...] + pltpu.roll(v, HEAD_WIDTH // 2, 1) * sin_s[...]

    for g in groups:
        ring2[g].near()
        ring3[g][3].begin()
        ring3[g][1].begin()
    for g in groups:
        ring2[g].finish()
        ring3[g][2].begin()
        share_mine(g, 0).start()

    sine = jnp.sin(angle)
    sin_s[...] = jnp.where(lane < HEAD_WIDTH // 2, -sine, sine)

    weights[0].wait()
    kv = jnp.dot(normed[...], wkv[...], preferred_element_type=jnp.float32)
    for h in range(2):
        k_s[h] = rotate(kv[:, h * 128:(h + 1) * 128]).astype(jnp.bfloat16)
        v_s[h] = kv[:, 256 + h * 128:256 + (h + 1) * 128].astype(jnp.bfloat16)

    owner = lax.broadcasted_iota(jnp.int32, (tokens, aqd.shape[1]), 1) // ADAPTER_RANK
    mine = owner == adapter_col
    weights[1].wait()
    inner = jnp.dot(normed[...], aqd[...], preferred_element_type=jnp.float32)
    inner_s[...] = jnp.where(mine, inner, 0.0).astype(jnp.bfloat16)
    weights[2].wait()
    weights[3].wait()

    def queries(lo, hi):
        @pl.loop(lo, hi)
        def _(n):
            cols = pl.ds(pl.multiple_of(n * 256, 256), 256)
            qv = jnp.dot(normed[...], wq[:, cols], preferred_element_type=jnp.float32)
            qv = qv + jnp.dot(inner_s[...], aqu[:, cols], preferred_element_type=jnp.float32)
            for h in range(2):
                q_s[n * 2 + h] = rotate(qv[:, h * 128:(h + 1) * 128]).astype(jnp.bfloat16)

    queries(0, 3)
    for g in groups:
        ring3[g][0].pass_on()
        for third in (0, 2):
            share_mine(g, 1 + third).start()
    queries(3, 6)

    row_i = lax.broadcasted_iota(jnp.int32, (tokens, tokens), 0)
    col_i = lax.broadcasted_iota(jnp.int32, (tokens, tokens), 1)
    rbuf[0] = jnp.full(rbuf.shape[1:], -1.0, jnp.float32)
    rbuf[0, 0:TOPK, :] = routes_ref[...].astype(jnp.float32)

    for o, before in ((3, 0), (1, 3), (2, 1)):
        for g in groups:
            ring3[g][o].pass_on()
            for third in (0, 2):
                share_mine(g, 1 + o * 3 + third).start()
            ring3[g][before].finish()
            share_mine(g, 1 + before * 3 + 1).start()
    r_copies = []
    for i, off in ((1, 1), (2, 3), (3, 2)):
        cp = remote(rbuf.at[0], rbuf.at[i], sa_r.at[i], ra_r.at[i], first_dev(off))
        cp.start()
        r_copies.append(cp)
    for g in groups:
        ring3[g][2].finish()
        share_mine(g, 1 + 2 * 3 + 1).start()
    for g in groups:
        for i in range(13):
            theirs(g, i).wait_recv()

    @pl.loop(0, 4)
    def _(r):
        base = prompt_ref[r] * PPP
        for j in range(PPP):
            page = table_ref[base + j]
            d = page // 4
            px, py, pz, pc = d // 32, lax.rem(d // 8, 4), lax.rem(d // 2, 4), lax.rem(d, 2)
            t = lax.rem(page, 4) * 4
            for col in range(4):
                kv_s[col, r, pl.ds(j * 16, 16), :] = cache[px, py, pz, pc, t + col]

    scale = HEAD_WIDTH ** (-0.5)
    group = QUERY_HEADS // KEY_VALUE_HEADS
    nt = (((1,), (1,)), ((), ()))

    before_m = jnp.where(row_i < col_i, 1.0, 0.0).astype(jnp.bfloat16)
    half = half_rows
    offsets = (0, 1, 3, 2)

    def x_copy(i, h):
        rows = pl.ds(h * half, half)
        return remote(xbuf.at[0, rows], xbuf.at[i, rows], sa_x.at[i, h], ra_x.at[i, h],
                      first_dev(offsets[i]))

    def attend(b):
        @pl.loop(0, KEY_VALUE_HEADS)
        def _(h):
            rows = slice(b * half_rows, (b + 1) * half_rows)
            keys = (b + 1) * half_rows
            q = q_s[pl.ds(h * group, group), rows, :].reshape(group * half_rows, HEAD_WIDTH)
            slot = slot_col[rows]
            ki = lax.broadcasted_iota(jnp.int32, (half_rows, keys), 1).astype(jnp.float32)
            ok = jnp.logical_and(ki <= index_col[rows], ki >= start_col[rows])
            local = lax.dot_general(q, k_s[h, 0:keys], nt, preferred_element_type=jnp.float32)
            local = local.reshape(group, half_rows, keys) * scale
            local = jnp.where(ok[None], local, VERY_NEGATIVE)
            picked = None
            for r in range(b, b + 3):
                s = lax.dot_general(q, kv_s[h, r], nt, preferred_element_type=jnp.float32)
                s = s.reshape(group, half_rows, PROMPT_LENGTH)
                picked = s if picked is None else jnp.where((slot == float(r))[None], s, picked)
            picked = picked * scale
            top = jnp.maximum(jnp.max(picked, axis=-1, keepdims=True), jnp.max(local, axis=-1, keepdims=True))
            wp = jnp.exp(picked - top)
            wl = jnp.exp(local - top)
            total = jnp.sum(wp, axis=-1, keepdims=True) + jnp.sum(wl, axis=-1, keepdims=True)
            wp = wp.astype(jnp.bfloat16).reshape(group * half_rows, PROMPT_LENGTH)
            wl = wl.astype(jnp.bfloat16).reshape(group * half_rows, keys)
            summed = None
            for r in range(b, b + 3):
                o = jnp.dot(wp, kv_s[KEY_VALUE_HEADS + h, r], preferred_element_type=jnp.float32)
                o = o.reshape(group, half_rows, HEAD_WIDTH)
                summed = o if summed is None else jnp.where((slot == float(r))[None], o, summed)
            o = jnp.dot(wl, v_s[h, 0:keys], preferred_element_type=jnp.float32)
            summed = (summed + o.reshape(group, half_rows, HEAD_WIDTH)) / total
            for i in range(group):
                col = pl.multiple_of((h * group + i) * HEAD_WIDTH, HEAD_WIDTH)
                att[rows, pl.ds(col, HEAD_WIDTH)] = summed[i].astype(jnp.bfloat16)

    def project(b):
        rows = slice(b * half_rows, (b + 1) * half_rows)
        inner = jnp.dot(att[rows], aod[...], preferred_element_type=jnp.float32)
        inner_s[rows] = jnp.where(mine[rows], inner, 0.0).astype(jnp.bfloat16)

        @pl.loop(0, width // 512)
        def _(n):
            cols = pl.ds(pl.multiple_of(n * 512, 512), 512)
            mix = jnp.dot(att[rows], wo[:, cols], preferred_element_type=jnp.float32)
            mix = mix + jnp.dot(inner_s[rows], aou[:, cols], preferred_element_type=jnp.float32)
            hid = (tokens_ref[rows, cols].astype(jnp.float32) + mix).astype(jnp.bfloat16)
            acc[rows, cols] = hid.astype(jnp.float32)

        hv = acc[rows]
        factor = lax.rsqrt(jnp.mean(hv * hv, axis=-1, keepdims=True) + EPSILON)
        xbuf[0, rows] = (hv * factor * expert_gain).astype(jnp.bfloat16)

    expert_gain = expert_gain_ref[...].astype(jnp.float32).reshape(1, width)
    attend(0)
    for cp in weights[4:7]:
        cp.wait()
    for b in range(2):
        if b:
            attend(b)
        project(b)
        x_copy(1, b).start()
        x_copy(2, b).start()

    experts = router_ref.shape[0]

    def make_tables(i):
        r = rbuf[i]
        ei = lax.broadcasted_iota(jnp.int32, (experts, tokens), 0).astype(jnp.float32)
        hit = ei == r[0:1, :]
        for k in range(1, TOPK):
            hit = jnp.logical_or(hit, ei == r[k:k + 1, :])
        hit_f = jnp.where(hit, 1.0, 0.0)
        rank = jnp.dot(hit_f.astype(jnp.bfloat16), before_m, preferred_element_type=jnp.float32)
        rank_s[i] = jnp.where(hit, rank, -1.0)
        logits = lax.dot_general(router_ref[...], xbuf[i], (((1,), (1,)), ((), ())),
                                 preferred_element_type=jnp.float32)
        sig = jnp.where(hit, jax.nn.sigmoid(logits), 0.0)
        gate_s[i] = sig / jnp.sum(sig, axis=0, keepdims=True)

    slot_i = lax.broadcasted_iota(jnp.int32, (CAP, tokens), 0).astype(jnp.float32)
    tile = 512

    def dispatch(i):
        picks = []
        for j in range(4):
            for dc in range(2):
                e = second_exp(j, dc)
                rank_row = rank_s[i, pl.ds(e, 1), :]
                gate_row = gate_s[i, pl.ds(e, 1), :]
                eq = slot_i == rank_row
                picks.append(jnp.where(eq, 1.0, 0.0).astype(jnp.bfloat16))
                q = j * 2 + dc
                ct_s[i, q * CAP:(q + 1) * CAP, :] = jnp.where(eq, gate_row, 0.0).astype(jnp.bfloat16)
        pick = jnp.concatenate(picks, axis=0)

        @pl.loop(0, width // tile)
        def _(n):
            cols = pl.ds(pl.multiple_of(n * tile, tile), tile)
            rows = jnp.dot(pick, xbuf[i, :, cols], preferred_element_type=jnp.float32).astype(jnp.bfloat16)
            arrived[i, 0:CAP, cols] = rows[0:CAP]
            pack[i * 8 * CAP:(i + 1) * 8 * CAP, cols] = rows
        for q in range(1, 8):
            pack_copy(i, q).start()

    def pack_copy(i, q):
        j, dc = q // 2, q % 2
        return remote(pack.at[pl.ds((i * 8 + q) * CAP, CAP)], arrived.at[i, pl.ds(q * CAP, CAP)],
                      sb_p.at[i, q], rb_p.at[i, q], (x, second_exp(j, dc)))

    def result_copy(i, q):
        j, dc = q // 2, q % 2
        return remote(result.at[pl.ds((i * 8 + q) * CAP, CAP)], returned.at[i, pl.ds(q * CAP, CAP)],
                      sb_r.at[i, q], rb_r.at[i, q], relay_dev(j, dc))

    def expert(i):
        for q in range(1, 8):
            pack_copy(i, q).wait_recv()

        @pl.loop(0, FFE // 256)
        def _(n):
            up_cols = pl.ds(pl.multiple_of(FFE + n * 256, 256), 256)
            cols = pl.ds(pl.multiple_of(n * 256, 256), 256)
            a = arrived[i]
            g = jnp.dot(a, wgu_ref[:, cols], preferred_element_type=jnp.float32)
            u = jnp.dot(a, wgu_ref[:, up_cols], preferred_element_type=jnp.float32)
            units[:, cols] = (jnp.maximum(g, 0.0) * u).astype(jnp.bfloat16)

        @pl.loop(0, width // tile)
        def _(n):
            cols = pl.ds(pl.multiple_of(n * tile, tile), tile)
            rows = jnp.dot(units[...], wdn_ref[:, cols], preferred_element_type=jnp.float32).astype(jnp.bfloat16)
            returned[i, 0:CAP, cols] = rows[0:CAP]
            result[i * 8 * CAP:(i + 1) * 8 * CAP, cols] = rows
        for q in range(1, 8):
            result_copy(i, q).start()

    def partial_copy(i):
        return remote(psend.at[i - 1], precv.at[i - 1], sp_s.at[i - 1], sp_r.at[i - 1],
                      first_dev(4 - offsets[i]))

    def combine(i):
        for q in range(1, 8):
            result_copy(i, q).wait_recv()

        @pl.loop(0, width // tile)
        def _(n):
            cols = pl.ds(pl.multiple_of(n * tile, tile), tile)
            part = lax.dot_general(ct_s[i], returned[i, :, cols], (((0,), (0,)), ((), ())),
                                   preferred_element_type=jnp.float32)
            if i == 0:
                acc[:, cols] = acc[:, cols] + part
            else:
                psend[i - 1, :, cols] = part.astype(jnp.bfloat16)
        if i:
            partial_copy(i).start()

    def forward(i):
        h = 0 if i == 1 else 1
        rows = pl.ds(h * half, half)
        return remote(xbuf.at[i, rows], xbuf.at[3, rows], sa_x.at[3, h], ra_x.at[3, h],
                      first_dev(1 if i == 1 else 3))

    make_tables(0)
    dispatch(0)
    for cp in weights[7:]:
        cp.wait()
    x_copy(1, 0).wait_recv()
    forward(1).start()
    x_copy(2, 1).wait_recv()
    forward(2).start()
    for i in (1, 2):
        r_copies[i - 1].wait_recv()
        x_copy(i, 1 if i == 1 else 0).wait_recv()
        make_tables(i)
        dispatch(i)
    expert(1)
    r_copies[2].wait_recv()
    forward(1).wait_recv()
    forward(2).wait_recv()
    make_tables(3)
    dispatch(3)
    expert(2)
    expert(3)
    combine(1)
    expert(0)
    combine(2)
    combine(3)
    partial_copy(1).wait_recv()
    acc[...] = acc[...] + precv[0].astype(jnp.float32)
    combine(0)
    partial_copy(2).wait_recv()
    acc[...] = acc[...] + precv[1].astype(jnp.float32)
    partial_copy(3).wait_recv()
    out_ref[...] = (acc[...] + precv[2].astype(jnp.float32)).astype(jnp.bfloat16)
    for cp in r_copies:
        cp.wait_send()
    for i in (1, 2):
        for h in range(2):
            x_copy(i, h).wait_send()
    forward(1).wait_send()
    forward(2).wait_send()
    for i in range(4):
        for q in range(1, 8):
            pack_copy(i, q).wait_send()
            result_copy(i, q).wait_send()
        if i:
            partial_copy(i).wait_send()
    for g in groups:
        ring1[g].drain()
        ring2[g].drain()
        for o in range(4):
            ring3[g][o].drain()
        for i in range(13):
            share_mine(g, i).wait_send()


def layer(slots, prompts, adapters, table, tokens, shard, gain, routes, expert_gain, router,
          wq, wkv, wo, aqd, aqu, aod, aou, wgu, wdn):
    rows, width = tokens.shape
    bf, f32 = jnp.bfloat16, jnp.float32
    dma = pltpu.SemaphoreType.DMA
    vmem = pl.BlockSpec(memory_space=pltpu.VMEM)
    smem = pl.BlockSpec(memory_space=pltpu.SMEM)
    hbm = pl.BlockSpec(memory_space=pl.ANY)
    experts = router.shape[1]
    ordered = (wq, wkv, aqd, aqu, wo, aod, aou, wgu.reshape(wgu.shape[-2:]), wdn.reshape(wdn.shape[-2:]))
    routed = 8 * CAP
    return pl.pallas_call(
        layer_kernel,
        out_shape=jax.ShapeDtypeStruct((rows, width), bf),
        in_specs=[vmem, smem, smem, smem, hbm, hbm, vmem, vmem, vmem, vmem] + [hbm] * 9,
        out_specs=vmem,
        scratch_shapes=[pltpu.VMEM((4, 4, 4, 2, 16, 16, 128), bf), pltpu.VMEM((rows, width), bf)]
        + [pltpu.VMEM(w.shape, bf) for w in ordered]
        + [
            pltpu.VMEM((rows, width), bf),
            pltpu.VMEM((rows, aqd.shape[1]), bf),
            pltpu.VMEM((rows, HEAD_WIDTH), f32),
            pltpu.VMEM((rows, HEAD_WIDTH), f32),
            pltpu.VMEM((QUERY_HEADS, rows, HEAD_WIDTH), bf),
            pltpu.VMEM((KEY_VALUE_HEADS, rows, HEAD_WIDTH), bf),
            pltpu.VMEM((KEY_VALUE_HEADS, rows, HEAD_WIDTH), bf),
            pltpu.VMEM((2 * KEY_VALUE_HEADS, 4, PROMPT_LENGTH, HEAD_WIDTH), bf),
            pltpu.VMEM((rows, width), bf),
            pltpu.VMEM((4, rows, width), bf),
            pltpu.VMEM((4, 8, rows), f32),
            pltpu.VMEM((4, experts, rows), f32),
            pltpu.VMEM((4, experts, rows), f32),
            pltpu.VMEM((4, routed, rows), bf),
            pltpu.VMEM((4, routed, width), bf),
            pltpu.VMEM((routed, FFE), bf),
            pltpu.VMEM((4, routed, width), bf),
            pltpu.VMEM((3, rows, width), bf),
            pltpu.VMEM((3, rows, width), bf),
            pltpu.VMEM((rows, width), f32),
            dma((10,)), dma((16,)), dma((3, 6, 5)), dma((3, 6, 5)), dma((3, 13)), dma((3, 13)),
            dma((4, 2)), dma((4, 2)), dma((4,)), dma((4,)),
            dma((4, 8)), dma((4, 8)), dma((4, 8)), dma((4, 8)),
            dma((3,)), dma((3,)),
        ],
        compiler_params=pltpu.CompilerParams(
            collective_id=1, has_side_effects=True, vmem_limit_bytes=63 * 1024 * 1024),
        name="layer",
    )(slots, prompts, adapters, table, tokens, shard, gain, routes.T, expert_gain, router.T, *ordered)


def on_device(
    tokens,
    token_request_slot,
    request_prompt,
    request_adapter,
    prompt_page_table,
    shared_prompt_cache,
    routes,
    attention_norm_gain,
    query_matrix,
    key_value_weight,
    attention_output_weight,
    adapter_query_down,
    adapter_query_up,
    adapter_output_down,
    adapter_output_up,
    expert_norm_gain,
    router,
    expert_gate_up,
    expert_down,
):
    return layer(
        token_request_slot, request_prompt, request_adapter, prompt_page_table, tokens,
        shared_prompt_cache, attention_norm_gain, routes, expert_norm_gain, router,
        query_matrix, key_value_weight, attention_output_weight, adapter_query_down,
        adapter_query_up, adapter_output_down, adapter_output_up, expert_gate_up, expert_down,
    )


def solution(mesh):
    return jax.shard_map(
        on_device,
        mesh=mesh,
        in_specs=(
            P(("req", "exp"), None),
            P(("req", "exp"), None),
            P(("req", "exp")),
            P(("req", "exp")),
            P(),
            P(("req", "exp"), None, None),
            P(("req", "exp"), None),
            P(),
            P(),
            P(),
            P(),
            P(),
            P(),
            P(),
            P(),
            P(),
            P(),
            P("exp", None, None),
            P("exp", None, None),
        ),
        out_specs=P(("req", "exp"), None),
        check_vma=False,
    )
```

```python
import math

import jax
import jax.numpy as jnp
from jax import lax
from jax.experimental import pallas as pl
from jax.experimental.pallas import tpu as pltpu
from jax.sharding import PartitionSpec as P

MESH = pl.DeviceIdType.MESH
CAP = 48
FFE = 768

QUERY_HEADS = 12
KEY_VALUE_HEADS = 2
HEAD_WIDTH = 128
TOPK = 4
ADAPTER_RANK = 16
PPP = 16
PROMPT_LENGTH = 256


EPSILON = 1e-06
THETA = 1000000.0
VERY_NEGATIVE = -1e30


TILE_GROUPS = ((0, 6), (6, 5), (11, 5))
AXIS_ORDERS = ((0, 1, 2), (1, 2, 0), (2, 0, 1))


def layer_kernel(
    slot_ref, prompt_ref, adapter_ref, table_ref, tokens_any, cache_ref, gain_ref,
    routes_ref, expert_gain_ref, router_ref,
    wq_any, wkv_any, aqd_any, aqu_any, wo_any, aod_any, aou_any, wgu_any, wdn_any,
    out_ref,
    cache, tokens_ref, wq, wkv, aqd, aqu, wo, aod, aou, wgu_ref, wdn_ref,
    normed, inner_s, cos_s, sin_s, q_s, k_s, v_s, kv_s, att,
    xbuf, rbuf, rank_s, gate_s, ct_s, arrived, units, returned, psend, precv, acc,
    w_sem, c_sem, ag_s, ag_r, co_s, co_r,
    sa_x, ra_x, sa_r, ra_r, sb_p, rb_p, sb_r, rb_r, sp_s, sp_r,
):
    pack, result = wo, wq
    x = lax.axis_index("req")
    e_me = lax.axis_index("exp")
    y = e_me // 8
    z = lax.rem(e_me // 2, 4)
    c = lax.rem(e_me, 2)
    here = (x, y, z)

    def device(axis, offset):
        p = list(here)
        p[axis] = lax.rem(p[axis] + offset, 4)
        return (p[0], (p[1] * 4 + p[2]) * 2 + c)

    partner = (x, (y * 4 + z) * 2 + 1 - c)

    barrier = pltpu.get_barrier_semaphore()
    for off in (1, 2, 3):
        pl.semaphore_signal(barrier, 1, device_id=device(0, off), device_id_type=MESH)
    for dy in range(4):
        for dc in range(2):
            if dy or dc:
                dev = (x, (lax.rem(y + dy, 4) * 4 + z) * 2 + lax.rem(c + dc, 2))
                pl.semaphore_signal(barrier, 1, device_id=dev, device_id_type=MESH)
    for dz in range(1, 4):
        for dc in range(2):
            dev = (x, (y * 4 + lax.rem(z + dz, 4)) * 2 + lax.rem(c + dc, 2))
            pl.semaphore_signal(barrier, 1, device_id=dev, device_id_type=MESH)

    first_pos = y * (1 - c) + z * c
    first_base = z * 2 * (1 - c) + y * 8 * c + c
    first_step = 8 - 6 * c
    second_pos = z * (1 - c) + y * c
    second_base = y * 8 * (1 - c) + z * 2 * c
    second_step = 2 + 6 * c

    def first_dev(offset):
        return (x, first_base + lax.rem(first_pos + offset, 4) * first_step)

    def second_exp(offset, dc):
        return second_base + lax.rem(second_pos + offset, 4) * second_step + lax.rem(c + dc, 2)

    def relay_dev(j, dc):
        rc = lax.rem(c + dc, 2)
        pos = z * (1 - rc) + y * rc
        base = y * 8 * (1 - rc) + z * 2 * rc
        return (x, base + lax.rem(pos - j + 4, 4) * (2 + 6 * rc) + rc)

    def remote(src, dst, ssem, rsem, dev):
        return pltpu.make_async_remote_copy(
            src_ref=src, dst_ref=dst, send_sem=ssem, recv_sem=rsem,
            device_id=dev, device_id_type=MESH)

    own = []
    for p in range(4):
        for col in range(4):
            cp = pltpu.make_async_copy(
                cache_ref.at[p, :, pl.ds(col * 128, 128)],
                cache.at[x, y, z, c, p * 4 + col], c_sem.at[p * 4 + col])
            cp.start()
            own.append(cp)
    token_copy = pltpu.make_async_copy(tokens_any, tokens_ref, w_sem.at[9])
    token_copy.start()
    weights = []
    for i, (src, dst) in enumerate((
            (wkv_any, wkv), (aqd_any, aqd), (aqu_any, aqu), (wq_any, wq),
            (aod_any, aod), (wo_any, wo), (aou_any, aou), (wgu_any, wgu_ref), (wdn_any, wdn_ref))):
        cp = pltpu.make_async_copy(src, dst, w_sem.at[i])
        cp.start()
        weights.append(cp)

    def block(where, first, count):
        return cache.at[where[0], where[1], where[2], c, pl.ds(first, count)]

    def step(g, phase, kind, axis, where):
        lo, n = TILE_GROUPS[g]
        if kind == 2:
            n = n // 2
        elif kind == 3:
            lo, n = lo + n // 2, n - n // 2
        view = block(where, lo, n)
        return pltpu.make_async_remote_copy(
            src_ref=view, dst_ref=view, send_sem=ag_s.at[g, phase, kind], recv_sem=ag_r.at[g, phase, kind],
            device_id=device(axis, {0: 1, 2: 1, 4: 2}.get(kind, 3)), device_id_type=MESH)

    every = slice(None)

    def place(g, second, third):
        order = AXIS_ORDERS[g]
        w = [every, every, every]
        for axis, off in ((order[1], second), (order[2], third)):
            if off is not None:
                w[axis] = lax.rem(here[axis] + off, 4)
        return w

    class Ring:
        def __init__(self, g, phase, axis, where_of):
            self.g, self.phase, self.axis, self.where_of = g, phase, axis, where_of

        def cp(self, kind, off):
            return step(self.g, self.phase, kind, self.axis, self.where_of(off))

        def begin(self):
            self.cp(0, 0).start()
            self.cp(1, 0).start()

        def pass_on(self):
            self.cp(0, 3).wait_recv()
            self.cp(2, 3).start()
            self.cp(1, 1).wait_recv()
            self.cp(3, 1).start()

        def finish(self):
            self.cp(2, 2).wait_recv()
            self.cp(3, 2).wait_recv()

        def drain(self):
            self.cp(0, 0).wait_send()
            self.cp(1, 0).wait_send()
            self.cp(2, 3).wait_send()
            self.cp(3, 1).wait_send()

    class Short(Ring):
        def begin(self):
            for kind in (0, 1, 4):
                self.cp(kind, 0).start()

        def near(self):
            self.cp(0, 3).wait_recv()
            self.cp(1, 1).wait_recv()

        def finish(self):
            self.cp(4, 2).wait_recv()

        def drain(self):
            for kind in (0, 1, 4):
                self.cp(kind, 0).wait_send()

    def first_where(g):
        def f(off):
            order = AXIS_ORDERS[g]
            w = [here[0], here[1], here[2]]
            w[order[0]] = lax.rem(here[order[0]] + off, 4)
            return w
        return f

    groups = range(3)
    ring1 = [Short(g, 0, AXIS_ORDERS[g][0], first_where(g)) for g in groups]
    ring2 = [Short(g, 1, AXIS_ORDERS[g][1], lambda off, g=g: place(g, off, 0)) for g in groups]
    ring3 = [[Ring(g, 2 + o, AXIS_ORDERS[g][2], lambda off, g=g, o=o: place(g, o, off)) for o in range(4)]
             for g in groups]

    def share(g, i, second, third):
        lo, n = TILE_GROUPS[g]
        view = block(place(g, second, third), lo, n)
        return pltpu.make_async_remote_copy(
            src_ref=view, dst_ref=view, send_sem=co_s.at[g, i], recv_sem=co_r.at[g, i],
            device_id=partner, device_id_type=MESH)

    def share_mine(g, i):
        if i == 0:
            return share(g, 0, None, 0)
        return share(g, i, (i - 1) // 3, 1 + (i - 1) % 3)

    def theirs(g, i):
        lo, n = TILE_GROUPS[g]
        second, third = (None, 0) if i == 0 else ((i - 1) // 3, 1 + (i - 1) % 3)
        w = place(g, second, third)
        view = cache.at[w[0], w[1], w[2], 1 - c, pl.ds(lo, n)]
        return pltpu.make_async_remote_copy(
            src_ref=view, dst_ref=view, send_sem=co_s.at[g, i], recv_sem=co_r.at[g, i],
            device_id=partner, device_id_type=MESH)

    tokens = tokens_ref.shape[0]
    width = tokens_ref.shape[1]
    half_rows = tokens // 2

    for cp in own:
        cp.wait()
    pl.semaphore_wait(barrier, 16)
    for g in groups:
        ring1[g].begin()

    token_copy.wait()
    tv = tokens_ref[...].astype(jnp.float32)
    factor = lax.rsqrt(jnp.mean(tv * tv, axis=-1, keepdims=True) + EPSILON)
    gain = gain_ref[...].astype(jnp.float32).reshape(1, width)
    normed[...] = (tv * factor * gain).astype(jnp.bfloat16)

    for g in groups:
        ring1[g].near()
        ring1[g].finish()
        ring2[g].begin()
    for g in groups:
        ring3[g][0].begin()

    slot_row = slot_ref[...]
    index_col = lax.broadcasted_iota(jnp.int32, (tokens, 1), 0).astype(jnp.float32)
    slot_col = jnp.zeros((tokens, 1), jnp.float32)
    start_col = jnp.zeros((tokens, 1), jnp.float32)
    adapter_col = jnp.zeros((tokens, 1), jnp.int32) + adapter_ref[0]
    for r in range(1, 4):
        start = jnp.sum(jnp.where(slot_row < r, 1.0, 0.0), axis=1, keepdims=True)
        reached = index_col >= start
        slot_col = jnp.where(reached, float(r), slot_col)
        start_col = jnp.where(reached, start, start_col)
        adapter_col = jnp.where(reached, adapter_ref[r], adapter_col)
    position = index_col - start_col + float(PROMPT_LENGTH)
    lane = lax.broadcasted_iota(jnp.int32, (1, HEAD_WIDTH), 1)
    pair = lax.rem(lane, HEAD_WIDTH // 2).astype(jnp.float32)
    frequency = jnp.exp(pair * (-math.log(THETA) / (HEAD_WIDTH // 2)))
    angle = position * frequency
    cos_s[...] = jnp.cos(angle)

    def rotate(v):
        return v * cos_s[...] + pltpu.roll(v, HEAD_WIDTH // 2, 1) * sin_s[...]

    for g in groups:
        ring2[g].near()
        ring3[g][3].begin()
        ring3[g][1].begin()
    for g in groups:
        ring2[g].finish()
        ring3[g][2].begin()
        share_mine(g, 0).start()

    sine = jnp.sin(angle)
    sin_s[...] = jnp.where(lane < HEAD_WIDTH // 2, -sine, sine)

    weights[0].wait()
    kv = jnp.dot(normed[...], wkv[...], preferred_element_type=jnp.float32)
    for h in range(2):
        k_s[h] = rotate(kv[:, h * 128:(h + 1) * 128]).astype(jnp.bfloat16)
        v_s[h] = kv[:, 256 + h * 128:256 + (h + 1) * 128].astype(jnp.bfloat16)

    owner = lax.broadcasted_iota(jnp.int32, (tokens, aqd.shape[1]), 1) // ADAPTER_RANK
    mine = owner == adapter_col
    weights[1].wait()
    inner = jnp.dot(normed[...], aqd[...], preferred_element_type=jnp.float32)
    inner_s[...] = jnp.where(mine, inner, 0.0).astype(jnp.bfloat16)
    weights[2].wait()
    weights[3].wait()

    def queries(lo, hi):
        @pl.loop(lo, hi)
        def _(n):
            cols = pl.ds(pl.multiple_of(n * 256, 256), 256)
            qv = jnp.dot(normed[...], wq[:, cols], preferred_element_type=jnp.float32)
            qv = qv + jnp.dot(inner_s[...], aqu[:, cols], preferred_element_type=jnp.float32)
            for h in range(2):
                q_s[n * 2 + h] = rotate(qv[:, h * 128:(h + 1) * 128]).astype(jnp.bfloat16)

    queries(0, 3)
    for g in groups:
        ring3[g][0].pass_on()
        for third in (0, 2):
            share_mine(g, 1 + third).start()
    queries(3, 6)

    row_i = lax.broadcasted_iota(jnp.int32, (tokens, tokens), 0)
    col_i = lax.broadcasted_iota(jnp.int32, (tokens, tokens), 1)
    rbuf[0] = jnp.full(rbuf.shape[1:], -1.0, jnp.float32)
    rbuf[0, 0:TOPK, :] = routes_ref[...].astype(jnp.float32)

    for o, before in ((3, 0), (1, 3), (2, 1)):
        for g in groups:
            ring3[g][o].pass_on()
            for third in (0, 2):
                share_mine(g, 1 + o * 3 + third).start()
            ring3[g][before].finish()
            share_mine(g, 1 + before * 3 + 1).start()
    r_copies = []
    for i, off in ((1, 1), (2, 3), (3, 2)):
        cp = remote(rbuf.at[0], rbuf.at[i], sa_r.at[i], ra_r.at[i], first_dev(off))
        cp.start()
        r_copies.append(cp)
    for g in groups:
        ring3[g][2].finish()
        share_mine(g, 1 + 2 * 3 + 1).start()
    for g in groups:
        for i in range(13):
            theirs(g, i).wait_recv()

    @pl.loop(0, 4)
    def _(r):
        base = prompt_ref[r] * PPP
        for j in range(PPP):
            page = table_ref[base + j]
            d = page // 4
            px, py, pz, pc = d // 32, lax.rem(d // 8, 4), lax.rem(d // 2, 4), lax.rem(d, 2)
            t = lax.rem(page, 4) * 4
            for col in range(4):
                kv_s[col, r, pl.ds(j * 16, 16), :] = cache[px, py, pz, pc, t + col]

    scale = HEAD_WIDTH ** (-0.5)
    group = QUERY_HEADS // KEY_VALUE_HEADS
    nt = (((1,), (1,)), ((), ()))

    before_m = jnp.where(row_i < col_i, 1.0, 0.0).astype(jnp.bfloat16)
    half = half_rows
    offsets = (0, 1, 3, 2)

    def x_copy(i, h):
        rows = pl.ds(h * half, half)
        return remote(xbuf.at[0, rows], xbuf.at[i, rows], sa_x.at[i, h], ra_x.at[i, h],
                      first_dev(offsets[i]))

    def attend(b):
        @pl.loop(0, KEY_VALUE_HEADS)
        def _(h):
            rows = slice(b * half_rows, (b + 1) * half_rows)
            keys = (b + 1) * half_rows
            q = q_s[pl.ds(h * group, group), rows, :].reshape(group * half_rows, HEAD_WIDTH)
            slot = slot_col[rows]
            ki = lax.broadcasted_iota(jnp.int32, (half_rows, keys), 1).astype(jnp.float32)
            ok = jnp.logical_and(ki <= index_col[rows], ki >= start_col[rows])
            local = lax.dot_general(q, k_s[h, 0:keys], nt, preferred_element_type=jnp.float32)
            local = local.reshape(group, half_rows, keys) * scale
            local = jnp.where(ok[None], local, VERY_NEGATIVE)
            picked = None
            for r in range(b, b + 3):
                s = lax.dot_general(q, kv_s[h, r], nt, preferred_element_type=jnp.float32)
                s = s.reshape(group, half_rows, PROMPT_LENGTH)
                picked = s if picked is None else jnp.where((slot == float(r))[None], s, picked)
            picked = picked * scale
            top = jnp.maximum(jnp.max(picked, axis=-1, keepdims=True), jnp.max(local, axis=-1, keepdims=True))
            wp = jnp.exp(picked - top)
            wl = jnp.exp(local - top)
            total = jnp.sum(wp, axis=-1, keepdims=True) + jnp.sum(wl, axis=-1, keepdims=True)
            wp = wp.astype(jnp.bfloat16).reshape(group * half_rows, PROMPT_LENGTH)
            wl = wl.astype(jnp.bfloat16).reshape(group * half_rows, keys)
            summed = None
            for r in range(b, b + 3):
                o = jnp.dot(wp, kv_s[KEY_VALUE_HEADS + h, r], preferred_element_type=jnp.float32)
                o = o.reshape(group, half_rows, HEAD_WIDTH)
                summed = o if summed is None else jnp.where((slot == float(r))[None], o, summed)
            o = jnp.dot(wl, v_s[h, 0:keys], preferred_element_type=jnp.float32)
            summed = (summed + o.reshape(group, half_rows, HEAD_WIDTH)) / total
            for i in range(group):
                col = pl.multiple_of((h * group + i) * HEAD_WIDTH, HEAD_WIDTH)
                att[rows, pl.ds(col, HEAD_WIDTH)] = summed[i].astype(jnp.bfloat16)

    def project(b):
        rows = slice(b * half_rows, (b + 1) * half_rows)
        inner = jnp.dot(att[rows], aod[...], preferred_element_type=jnp.float32)
        inner_s[rows] = jnp.where(mine[rows], inner, 0.0).astype(jnp.bfloat16)

        @pl.loop(0, width // 512)
        def _(n):
            cols = pl.ds(pl.multiple_of(n * 512, 512), 512)
            mix = jnp.dot(att[rows], wo[:, cols], preferred_element_type=jnp.float32)
            mix = mix + jnp.dot(inner_s[rows], aou[:, cols], preferred_element_type=jnp.float32)
            hid = (tokens_ref[rows, cols].astype(jnp.float32) + mix).astype(jnp.bfloat16)
            acc[rows, cols] = hid.astype(jnp.float32)

        hv = acc[rows]
        factor = lax.rsqrt(jnp.mean(hv * hv, axis=-1, keepdims=True) + EPSILON)
        xbuf[0, rows] = (hv * factor * expert_gain).astype(jnp.bfloat16)

    expert_gain = expert_gain_ref[...].astype(jnp.float32).reshape(1, width)
    attend(0)
    for cp in weights[4:7]:
        cp.wait()
    for b in range(2):
        if b:
            attend(b)
        project(b)
        x_copy(1, b).start()
        x_copy(2, b).start()

    experts = router_ref.shape[0]

    def make_tables(i):
        r = rbuf[i]
        ei = lax.broadcasted_iota(jnp.int32, (experts, tokens), 0).astype(jnp.float32)
        hit = ei == r[0:1, :]
        for k in range(1, TOPK):
            hit = jnp.logical_or(hit, ei == r[k:k + 1, :])
        hit_f = jnp.where(hit, 1.0, 0.0)
        rank = jnp.dot(hit_f.astype(jnp.bfloat16), before_m, preferred_element_type=jnp.float32)
        rank_s[i] = jnp.where(hit, rank, -1.0)
        logits = lax.dot_general(router_ref[...], xbuf[i], (((1,), (1,)), ((), ())),
                                 preferred_element_type=jnp.float32)
        sig = jnp.where(hit, jax.nn.sigmoid(logits), 0.0)
        gate_s[i] = sig / jnp.sum(sig, axis=0, keepdims=True)

    slot_i = lax.broadcasted_iota(jnp.int32, (CAP, tokens), 0).astype(jnp.float32)
    tile = 512

    def dispatch(i):
        picks = []
        for j in range(4):
            for dc in range(2):
                e = second_exp(j, dc)
                rank_row = rank_s[i, pl.ds(e, 1), :]
                gate_row = gate_s[i, pl.ds(e, 1), :]
                eq = slot_i == rank_row
                picks.append(jnp.where(eq, 1.0, 0.0).astype(jnp.bfloat16))
                q = j * 2 + dc
                ct_s[i, q * CAP:(q + 1) * CAP, :] = jnp.where(eq, gate_row, 0.0).astype(jnp.bfloat16)
        pick = jnp.concatenate(picks, axis=0)

        @pl.loop(0, width // tile)
        def _(n):
            cols = pl.ds(pl.multiple_of(n * tile, tile), tile)
            rows = jnp.dot(pick, xbuf[i, :, cols], preferred_element_type=jnp.float32).astype(jnp.bfloat16)
            arrived[i, 0:CAP, cols] = rows[0:CAP]
            pack[i * 8 * CAP:(i + 1) * 8 * CAP, cols] = rows
        for q in range(1, 8):
            pack_copy(i, q).start()

    def pack_copy(i, q):
        j, dc = q // 2, q % 2
        return remote(pack.at[pl.ds((i * 8 + q) * CAP, CAP)], arrived.at[i, pl.ds(q * CAP, CAP)],
                      sb_p.at[i, q], rb_p.at[i, q], (x, second_exp(j, dc)))

    def tile_columns(n):
        return pl.ds(pl.multiple_of(n * tile, tile), tile)

    def result_copy(i, q, n):
        j, dc = q // 2, q % 2
        cols = tile_columns(n)
        return remote(result.at[pl.ds((i * 8 + q) * CAP, CAP), cols],
                      returned.at[i, pl.ds(q * CAP, CAP), cols],
                      sb_r.at[i, q, n], rb_r.at[i, q, n], relay_dev(j, dc))

    def expert(i):
        for q in range(1, 8):
            pack_copy(i, q).wait_recv()

        @pl.loop(0, FFE // 256)
        def _(n):
            up_cols = pl.ds(pl.multiple_of(FFE + n * 256, 256), 256)
            cols = pl.ds(pl.multiple_of(n * 256, 256), 256)
            a = arrived[i]
            g = jnp.dot(a, wgu_ref[:, cols], preferred_element_type=jnp.float32)
            u = jnp.dot(a, wgu_ref[:, up_cols], preferred_element_type=jnp.float32)
            units[:, cols] = (jnp.maximum(g, 0.0) * u).astype(jnp.bfloat16)

        @pl.loop(0, width // tile)
        def _(n):
            cols = pl.ds(pl.multiple_of(n * tile, tile), tile)
            rows = jnp.dot(units[...], wdn_ref[:, cols], preferred_element_type=jnp.float32).astype(jnp.bfloat16)
            returned[i, 0:CAP, cols] = rows[0:CAP]
            result[i * 8 * CAP:(i + 1) * 8 * CAP, cols] = rows
            for q in range(1, 8):
                result_copy(i, q, n).start()

    def partial_copy(i, n):
        cols = tile_columns(n)
        return remote(psend.at[i - 1, :, cols], precv.at[i - 1, :, cols],
                      sp_s.at[i - 1, n], sp_r.at[i - 1, n], first_dev(4 - offsets[i]))

    def far_copy(h, n):
        rows, cols = pl.ds(h * half, half), tile_columns(n)
        return remote(psend.at[2, rows, cols], precv.at[2, rows, cols],
                      sp_s.at[2 + h, n], sp_r.at[2 + h, n], first_dev(3 if h == 0 else 1))

    def combine(i):
        @pl.loop(0, width // tile)
        def _(n):
            cols = tile_columns(n)
            for q in range(1, 8):
                result_copy(i, q, n).wait_recv()
            part = lax.dot_general(ct_s[i], returned[i, :, cols], (((0,), (0,)), ((), ())),
                                   preferred_element_type=jnp.float32)
            if i == 0:
                acc[:, cols] = acc[:, cols] + part
            elif i == 3:
                psend[2, :, cols] = part.astype(jnp.bfloat16)
                far_copy(0, n).start()
                far_copy(1, n).start()
            else:
                rows = slice((i - 1) * half, i * half)
                rest = slice((2 - i) * half, (3 - i) * half)
                far_copy(i - 1, n).wait_recv()
                passed = precv[2, rows, cols].astype(jnp.float32)
                psend[i - 1, rows, cols] = (part[rows] + passed).astype(jnp.bfloat16)
                psend[i - 1, rest, cols] = part[rest].astype(jnp.bfloat16)
                partial_copy(i, n).start()

    def forward(i):
        h = 0 if i == 1 else 1
        rows = pl.ds(h * half, half)
        return remote(xbuf.at[i, rows], xbuf.at[3, rows], sa_x.at[3, h], ra_x.at[3, h],
                      first_dev(1 if i == 1 else 3))

    make_tables(0)
    dispatch(0)
    for cp in weights[7:]:
        cp.wait()
    x_copy(1, 0).wait_recv()
    forward(1).start()
    x_copy(2, 1).wait_recv()
    forward(2).start()
    for i in (1, 2):
        r_copies[i - 1].wait_recv()
        x_copy(i, 1 if i == 1 else 0).wait_recv()
        make_tables(i)
        dispatch(i)
    expert(1)
    r_copies[2].wait_recv()
    forward(1).wait_recv()
    forward(2).wait_recv()
    make_tables(3)
    dispatch(3)
    expert(3)
    expert(2)
    combine(3)
    expert(0)
    combine(1)
    combine(2)
    def receive(i):
        @pl.loop(0, width // tile)
        def _(n):
            cols = tile_columns(n)
            partial_copy(i, n).wait_recv()
            total = acc[:, cols] + precv[i - 1, :, cols].astype(jnp.float32)
            if i < 2:
                acc[:, cols] = total
            else:
                out_ref[:, cols] = total.astype(jnp.bfloat16)

    combine(0)
    receive(1)
    receive(2)
    for cp in r_copies:
        cp.wait_send()
    for i in (1, 2):
        for h in range(2):
            x_copy(i, h).wait_send()
    forward(1).wait_send()
    forward(2).wait_send()
    for i in range(4):
        for q in range(1, 8):
            pack_copy(i, q).wait_send()

        @pl.loop(0, width // tile)
        def _(n):
            for q in range(1, 8):
                result_copy(i, q, n).wait_send()
            if i in (1, 2):
                partial_copy(i, n).wait_send()
                far_copy(i - 1, n).wait_send()
    for g in groups:
        ring1[g].drain()
        ring2[g].drain()
        for o in range(4):
            ring3[g][o].drain()
        for i in range(13):
            share_mine(g, i).wait_send()


def layer(slots, prompts, adapters, table, tokens, shard, gain, routes, expert_gain, router,
          wq, wkv, wo, aqd, aqu, aod, aou, wgu, wdn):
    rows, width = tokens.shape
    bf, f32 = jnp.bfloat16, jnp.float32
    dma = pltpu.SemaphoreType.DMA
    vmem = pl.BlockSpec(memory_space=pltpu.VMEM)
    smem = pl.BlockSpec(memory_space=pltpu.SMEM)
    hbm = pl.BlockSpec(memory_space=pl.ANY)
    experts = router.shape[1]
    ordered = (wq, wkv, aqd, aqu, wo, aod, aou, wgu.reshape(wgu.shape[-2:]), wdn.reshape(wdn.shape[-2:]))
    routed = 8 * CAP
    return pl.pallas_call(
        layer_kernel,
        out_shape=jax.ShapeDtypeStruct((rows, width), bf),
        in_specs=[vmem, smem, smem, smem, hbm, hbm, vmem, vmem, vmem, vmem] + [hbm] * 9,
        out_specs=vmem,
        scratch_shapes=[pltpu.VMEM((4, 4, 4, 2, 16, 16, 128), bf), pltpu.VMEM((rows, width), bf)]
        + [pltpu.VMEM(w.shape, bf) for w in ordered]
        + [
            pltpu.VMEM((rows, width), bf),
            pltpu.VMEM((rows, aqd.shape[1]), bf),
            pltpu.VMEM((rows, HEAD_WIDTH), f32),
            pltpu.VMEM((rows, HEAD_WIDTH), f32),
            pltpu.VMEM((QUERY_HEADS, rows, HEAD_WIDTH), bf),
            pltpu.VMEM((KEY_VALUE_HEADS, rows, HEAD_WIDTH), bf),
            pltpu.VMEM((KEY_VALUE_HEADS, rows, HEAD_WIDTH), bf),
            pltpu.VMEM((2 * KEY_VALUE_HEADS, 4, PROMPT_LENGTH, HEAD_WIDTH), bf),
            pltpu.VMEM((rows, width), bf),
            pltpu.VMEM((4, rows, width), bf),
            pltpu.VMEM((4, 8, rows), f32),
            pltpu.VMEM((4, experts, rows), f32),
            pltpu.VMEM((4, experts, rows), f32),
            pltpu.VMEM((4, routed, rows), bf),
            pltpu.VMEM((4, routed, width), bf),
            pltpu.VMEM((routed, FFE), bf),
            pltpu.VMEM((4, routed, width), bf),
            pltpu.VMEM((3, rows, width), bf),
            pltpu.VMEM((3, rows, width), bf),
            pltpu.VMEM((rows, width), f32),
            dma((10,)), dma((16,)), dma((3, 6, 5)), dma((3, 6, 5)), dma((3, 13)), dma((3, 13)),
            dma((4, 2)), dma((4, 2)), dma((4,)), dma((4,)),
            dma((4, 8)), dma((4, 8)), dma((4, 8, 3)), dma((4, 8, 3)),
            dma((4, 3)), dma((4, 3)),
        ],
        compiler_params=pltpu.CompilerParams(
            collective_id=1, has_side_effects=True, vmem_limit_bytes=63 * 1024 * 1024),
        name="layer",
    )(slots, prompts, adapters, table, tokens, shard, gain, routes.T, expert_gain, router.T, *ordered)


def on_device(
    tokens,
    token_request_slot,
    request_prompt,
    request_adapter,
    prompt_page_table,
    shared_prompt_cache,
    routes,
    attention_norm_gain,
    query_matrix,
    key_value_weight,
    attention_output_weight,
    adapter_query_down,
    adapter_query_up,
    adapter_output_down,
    adapter_output_up,
    expert_norm_gain,
    router,
    expert_gate_up,
    expert_down,
):
    return layer(
        token_request_slot, request_prompt, request_adapter, prompt_page_table, tokens,
        shared_prompt_cache, attention_norm_gain, routes, expert_norm_gain, router,
        query_matrix, key_value_weight, attention_output_weight, adapter_query_down,
        adapter_query_up, adapter_output_down, adapter_output_up, expert_gate_up, expert_down,
    )


def solution(mesh):
    return jax.shard_map(
        on_device,
        mesh=mesh,
        in_specs=(
            P(("req", "exp"), None),
            P(("req", "exp"), None),
            P(("req", "exp")),
            P(("req", "exp")),
            P(),
            P(("req", "exp"), None, None),
            P(("req", "exp"), None),
            P(),
            P(),
            P(),
            P(),
            P(),
            P(),
            P(),
            P(),
            P(),
            P(),
            P("exp", None, None),
            P("exp", None, None),
        ),
        out_specs=P(("req", "exp"), None),
        check_vma=False,
    )
```
